512 devices in a mesh: blk: 8 (over z_hi, core), win: 64 (over x, y, z_lo).
Axes of the slice: x: 4, y: 8, z: 8 (z_hi: 4, z_lo: 2; z = z_hi * 2 + z_lo), core: 2. Of those that a mesh axis runs over, the one named last changes fastest.
Arguments:
- frame_tokens: bfloat16 [8, 64, 128, 1024], P('blk', 'win'), may hold values from -21 to 21, as said below
- w_kv: bfloat16 [1024, 2048], replicated, may hold values from -0.1875 to 0.1875
- w_q: bfloat16 [1024, 1024], P('win'), may hold values from -0.1875 to 0.1875
- w_out: bfloat16 [1024, 1024], P('win'), may hold values from -0.1875 to 0.1875
- slot_tokens: int32 [8, 64, 128], P(None, 'win'), may hold values from 0 to 1023, as said below
- counts: int32 [8, 64], P('blk', 'win'), may hold values from 32 to 128, as said below
Outputs:
- projected: bfloat16 [8, 64, 128, 1024], P('blk', 'win')
The draws below stay inside these ranges and needn't reach their ends.
Inputs may be any that keep to these rules, and one draw needn't show every extreme that they name: `frame_tokens`: shown draw: a normal law truncated at 6. `slot_tokens`: every slot names a token of its own window. For each frame group and window the 128 slots name tokens of exactly 4 frames, 32 from each; no token of a window is named twice. `counts`: slots below the count are live. Each window has a frame group with all 128 slots live.
All inputs are finite; a program needn't handle non-finite values.
Results may differ from the reference program's by a relative error of at most 0.012.
The reference program's roundings to bfloat16 on the way count: a program that leaves them out, or rounds other values in their place, can miss the bound.
Values may be sent and summed in bfloat16 or wider, within the bound.
A program may use at most 64 MiB of HBM per device.

```python
import jax
import jax.numpy as jnp
from jax import lax

D = 1024
HEADS = 16
P_SIZE = 128
QS = 128
FRAMES = 8
WINDOWS = 64


def draw_frame_tokens(key, part):
    full_shape = (FRAMES, WINDOWS, P_SIZE, D)
    return jax.random.truncated_normal(key, -6.0, 6.0, full_shape, jnp.float32).astype(jnp.bfloat16)


def draw_slot_tokens(key, part):
    groups = FRAMES
    share_count = min(4, groups)
    per_owner = QS // share_count
    cycle_key, token_key, shuffle_key = jax.random.split(jax.random.fold_in(key, 11), 3)
    cycle_keys = jax.random.split(cycle_key, WINDOWS)
    order_in = jax.vmap(lambda one_key: jax.random.permutation(one_key, groups))(cycle_keys).astype(jnp.int32)
    position = jnp.argsort(order_in, axis=1).astype(jnp.int32)
    token_keys = jax.random.split(token_key, WINDOWS * groups)
    token_perm = jax.vmap(lambda one_key: jax.random.permutation(one_key, P_SIZE))(token_keys).astype(jnp.int32)
    slot_index = jnp.arange(QS, dtype=jnp.int32)
    step_of = slot_index // per_owner
    cycle_index = (position.T[:, :, None] + step_of[None, None, :]) % groups
    owner_of = jnp.take_along_axis(jnp.broadcast_to(order_in[None, :, :], (groups, WINDOWS, groups)), cycle_index, axis=2)
    window_of = jnp.arange(WINDOWS, dtype=jnp.int32)[None, :, None]
    flat_index = (window_of * groups + owner_of) * P_SIZE + slot_index[None, None, :]
    base_picks = owner_of * P_SIZE + token_perm.reshape(-1)[flat_index]
    shuffle_keys = jax.random.split(shuffle_key, groups * WINDOWS)
    slot_perm = jax.vmap(lambda one_key: jax.random.permutation(one_key, QS))(shuffle_keys).astype(jnp.int32)
    return jnp.take_along_axis(base_picks, slot_perm.reshape(groups, WINDOWS, QS), axis=2).astype(jnp.int32)


def draw_counts(key, part):
    first_key, second_key = jax.random.split(jax.random.fold_in(key, 23))
    low_counts = jax.random.randint(first_key, (FRAMES, WINDOWS), QS // 4, QS + 1)
    full_group = jax.random.randint(second_key, (WINDOWS,), 0, FRAMES)
    frame_index = jnp.arange(FRAMES, dtype=jnp.int32)[:, None]
    return jnp.where(frame_index == full_group[None, :], QS, low_counts).astype(jnp.int32)


def block_levels(stream_key, shape, pieces, low, top_value):
    gain = 1.0
    for dim, parts in pieces:
        heights = jax.random.uniform(jax.random.fold_in(jax.random.fold_in(stream_key, 6), dim), (parts,), jnp.float32, low / len(pieces), top_value / len(pieces))
        gain = gain * jnp.repeat(jnp.exp(heights), shape[dim] // parts).reshape((-1,) + (1,) * (len(shape) - 1 - dim))
    return gain


def bell_draw(key, extent, deviation, reach, cuts=(), kind=jnp.bfloat16):
    values = deviation * jax.random.normal(key, extent, jnp.float32)
    if cuts:
        values = values * block_levels(key, extent, cuts, -0.22, 0.18)
    return jnp.clip(values, -reach, reach).astype(kind)


def setup_inputs(seed: int = 0) -> dict:
    arg_keys = jax.random.split(jax.random.key(seed), 7)
    frame_tokens = draw_frame_tokens(jax.random.fold_in(arg_keys[6], 71), 0)
    w_kv = bell_draw(arg_keys[1], (D, 2 * D), D ** -0.5, 0.1875)
    w_q = bell_draw(arg_keys[2], (D, D), D ** -0.5, 0.1875, ((0, 64),))
    w_out = bell_draw(arg_keys[3], (D, D), D ** -0.5, 0.1875, ((0, 64),))
    slot_tokens = draw_slot_tokens(jax.random.fold_in(arg_keys[6], 71), 0)
    counts = draw_counts(jax.random.fold_in(arg_keys[6], 71), 0)
    return {"frame_tokens": frame_tokens, "w_kv": w_kv, "w_q": w_q, "w_out": w_out, "slot_tokens": slot_tokens, "counts": counts}


def attend_window(window_tokens, slot_rows, live_mask, w_kv, w_q, w_out):
    flat_rows = window_tokens.reshape(-1, D)
    key_value = jnp.dot(flat_rows, w_kv, preferred_element_type=jnp.float32).astype(jnp.bfloat16)
    key_rows = key_value[:, :D]
    value_rows = key_value[:, D:]
    picked = flat_rows[slot_rows.reshape(-1)]
    query_rows = jnp.dot(picked, w_q, preferred_element_type=jnp.float32).astype(jnp.bfloat16)
    head_dim = D // HEADS
    query_heads = query_rows.reshape(-1, HEADS, head_dim).astype(jnp.float32)
    key_heads = key_rows.reshape(-1, HEADS, head_dim).astype(jnp.float32)
    value_heads = value_rows.reshape(-1, HEADS, head_dim).astype(jnp.float32)
    scores = jnp.einsum("shd,khd->hsk", query_heads, key_heads) * (head_dim ** -0.5)
    row_peak = jnp.max(scores, axis=-1, keepdims=True)
    raw_weights = jnp.exp(scores - row_peak)
    total_sum = jnp.sum(raw_weights, axis=-1)
    weights = raw_weights.astype(jnp.bfloat16)
    mixed_rows = jnp.einsum("hsk,khd->shd", weights.astype(jnp.float32), value_heads)
    attended = (mixed_rows / total_sum.T[:, :, None]).astype(jnp.bfloat16).reshape(-1, D)
    out_sum = jnp.dot(attended, w_out, preferred_element_type=jnp.float32) * live_mask.reshape(-1, 1)
    return out_sum.astype(jnp.bfloat16).reshape(slot_rows.shape[0], QS, D)


def reference(frame_tokens, w_kv, w_q, w_out, slot_tokens, counts):
    live_mask = (jnp.arange(QS, dtype=jnp.int32)[None, None, :] < counts[:, :, None]).astype(jnp.float32)
    by_window = jnp.transpose(frame_tokens, (1, 0, 2, 3))
    slot_table = jnp.transpose(slot_tokens, (1, 0, 2))
    live_table = jnp.transpose(live_mask, (1, 0, 2))

    def one_window(packed):
        return attend_window(packed[0], packed[1], packed[2], w_kv, w_q, w_out)

    results = lax.map(one_window, (by_window, slot_table, live_table))
    return jnp.transpose(results, (1, 0, 2, 3))
```

```python
import functools

import jax
import jax.numpy as jnp
from jax import lax
from jax.experimental import pallas as pl
from jax.experimental.pallas import tpu as pltpu
from jax.sharding import PartitionSpec as P

HEADS = 16
NX, NY, NZ = 4, 8, 4
MESH = pl.DeviceIdType.MESH
F32 = jnp.float32
BF16 = jnp.bfloat16

NAMES = ["tp0", "tp1", "tm0", "tm1", "tf0", "tf1", "ts1", "ts4", "ts5", "ts70", "ts71"]
for _i in range(2):
    NAMES += [f"pair{_i}"]
    NAMES += [f"yo{_i}{_d}" for _d in range(1, NY)] + [f"yp{_i}{_d}" for _d in range(1, NY)]
    NAMES += [f"x{_k}{_i}" for _k in ("p0", "p1", "m0", "m1", "f0", "f1", "s0", "sm", "sp", "so")]
INDEX = {name: at for at, name in enumerate(NAMES)}


def kernel(tok_in, wkv_in, wq_in, wo_in, slots_ref, counts_ref, out_ref,
           tok, wkv, wq, wo, kv, qs, att, picked, send, recv, near):
    b = lax.axis_index("blk")
    w = lax.axis_index("win")
    core, zh = lax.rem(b, 2), b // 2
    zl, y, x = lax.rem(w, 2), lax.rem(w // 2, NY), w // (2 * NY)

    def at_blk(z, c):
        return (lax.rem(z + NZ, NZ) * 2 + c, w)

    def at_win(xx, yy, zz):
        return (b, (lax.rem(xx + NX, NX) * NY + lax.rem(yy, NY)) * 2 + zz)

    sib = (b + 1 - 2 * core, w)
    zp, zm = at_blk(zh + 1, core), at_blk(zh - 1, core)
    pair = at_win(x, y, 1 - zl)
    xp, xm = at_win(x + 1, y, zl), at_win(x - 1, y, zl)
    peers = [at_win(x, y + d, zl) for d in range(1, NY)]

    started = []

    def move(name, src, dst, device):
        copy = pltpu.make_async_remote_copy(
            src_ref=src, dst_ref=dst, send_sem=send.at[INDEX[name]], recv_sem=recv.at[INDEX[name]],
            device_id=device, device_id_type=MESH,
        )
        copy.start()
        started.append(copy)

    def got(name, dst):
        pltpu.make_async_remote_copy(
            src_ref=dst, dst_ref=dst, send_sem=send.at[INDEX[name]], recv_sem=recv.at[INDEX[name]],
            device_id=sib, device_id_type=MESH,
        ).wait_recv()

    barrier = pltpu.get_barrier_semaphore()
    everyone = [sib, zp, zm, pair, xp, xm] + peers
    for device in everyone:
        pl.semaphore_signal(barrier, inc=1, device_id=device, device_id_type=MESH)
    load_tok = pltpu.make_async_copy(tok_in.at[0, 0], tok.at[0], near.at[0])
    load_tok.start()
    load_kv = pltpu.make_async_copy(wkv_in, wkv, near.at[1])
    load_kv.start()
    cols = pl.ds(pl.multiple_of(core * 512, 512), 512)
    mine = pl.ds(pl.multiple_of(y * 32 + zl * 16, 16), 16)
    other = pl.ds(pl.multiple_of(y * 32 + (1 - zl) * 16, 16), 16)
    weights = ((0, wq_in, wq), (1, wo_in, wo))
    loads = []
    for i, src, buf in weights:
        copy = pltpu.make_async_copy(src.at[:, cols], buf.at[x, mine, cols], near.at[2 + i])
        copy.start()
        loads.append(copy)
    pl.semaphore_wait(barrier, len(everyone))

    def half(h):
        return pl.ds(64 * h, 64)

    def upper(h):
        return pl.ds(128 * h, 128)

    for i, src, buf in weights:
        move(f"pair{i}", src.at[:, cols], buf.at[x, mine, cols], pair)
    move("tp0", tok_in.at[0, 0, half(0)], tok.at[2, half(0)], zp)
    move("tm1", tok_in.at[0, 0, half(1)], tok.at[3, half(1)], zm)
    move("tp1", tok_in.at[0, 0, half(1)], tok.at[2, half(1)], zp)
    move("tm0", tok_in.at[0, 0, half(0)], tok.at[3, half(0)], zm)
    move("ts1", tok_in.at[0, 0], tok.at[1], sib)
    for i, src, buf in weights:
        for d in range(1, NY):
            move(f"yo{i}{d}", src.at[:, cols], buf.at[x, mine, cols], peers[d - 1])
        if i == 0:
            for k, _, buf2 in weights:
                got(f"pair{k}", buf2.at[x, other, cols])
        for d in range(1, NY):
            move(f"yp{i}{d}", buf.at[x, other, cols], buf.at[x, other, cols], peers[d - 1])

    def slab(buf, k, h=None):
        if h is None:
            return buf.at[lax.rem(x + k + NX, NX), :, cols]
        return buf.at[lax.rem(x + k + NX, NX), upper(h), cols]

    def wait_y(i, buf):
        loads[i].wait()
        for d in range(1, NY):
            yy = lax.rem(y + NY - d, NY)
            got(f"yo{i}{d}", buf.at[x, pl.ds(pl.multiple_of(yy * 32 + zl * 16, 16), 16), cols])
            got(f"yp{i}{d}", buf.at[x, pl.ds(pl.multiple_of(yy * 32 + (1 - zl) * 16, 16), 16), cols])
        move(f"xp0{i}", slab(buf, 0, 0), slab(buf, 0, 0), xp)
        move(f"xm1{i}", slab(buf, 0, 1), slab(buf, 0, 1), xm)
        move(f"xp1{i}", slab(buf, 0, 1), slab(buf, 0, 1), xp)
        move(f"xm0{i}", slab(buf, 0, 0), slab(buf, 0, 0), xm)
        move(f"xs0{i}", slab(buf, 0), slab(buf, 0), sib)

    def wait_x1(i, buf):
        got(f"xp0{i}", slab(buf, -1, 0))
        move(f"xf0{i}", slab(buf, -1, 0), slab(buf, -1, 0), xp)
        got(f"xm1{i}", slab(buf, 1, 1))
        move(f"xf1{i}", slab(buf, 1, 1), slab(buf, 1, 1), xm)

    def wait_x2(i, buf):
        got(f"xp1{i}", slab(buf, -1, 1))
        move(f"xsm{i}", slab(buf, -1), slab(buf, -1), sib)
        got(f"xm0{i}", slab(buf, 1, 0))
        move(f"xsp{i}", slab(buf, 1), slab(buf, 1), sib)

    def wait_x3(i, buf):
        got(f"xf0{i}", slab(buf, 2, 0))
        got(f"xf1{i}", slab(buf, 2, 1))
        move(f"xso{i}", slab(buf, 2), slab(buf, 2), sib)

    other_cols = pl.ds(pl.multiple_of((1 - core) * 512, 512), 512)

    def wait_s(i, buf):
        for k, name in ((0, "xs0"), (-1, "xsm"), (1, "xsp"), (2, "xso")):
            got(f"{name}{i}", buf.at[lax.rem(x + k + NX, NX), :, other_cols])

    def make_kv(j):
        rows = tok[pl.ds(j, 2)].reshape(256, 1024)

        @pl.loop(0, 4)
        def _(n):
            at = pl.ds(pl.multiple_of(n * 512, 512), 512)
            kv[pl.ds(128 * j, 256), at] = jnp.dot(rows, wkv[:, at], preferred_element_type=F32).astype(BF16)

    frames = [b, b + 1 - 2 * core, zm[0], zp[0], zm[0] + 1 - 2 * core, zp[0] + 1 - 2 * core]
    opposite = lax.rem(zh + 2, NZ) * 2 + core
    frames += [opposite, opposite + 1 - 2 * core]
    wanted = slots_ref[pl.ds(b, 1), 0, :]

    def pick(j):
        hits = []
        for k in (j, j + 1):
            token = lax.broadcasted_iota(jnp.int32, (128, 128), 0) + frames[k] * 128
            hits.append(jnp.where(token == wanted, 1.0, 0.0).T.astype(BF16))
        rows = tok[pl.ds(j, 2)].reshape(256, 1024)
        part = jnp.dot(jnp.concatenate(hits, axis=1), rows, preferred_element_type=F32)
        if j == 0:
            picked[...] = part
        else:
            picked[...] += part

    load_tok.wait()
    load_kv.wait()
    got("ts1", tok.at[1])
    make_kv(0)
    pick(0)
    got("tp0", tok.at[2, half(0)])
    move("tf0", tok.at[2, half(0)], tok.at[6, half(0)], zp)
    got("tm1", tok.at[3, half(1)])
    move("tf1", tok.at[3, half(1)], tok.at[6, half(1)], zm)
    wait_y(0, wq)
    got("tp1", tok.at[2, half(1)])
    move("ts4", tok.at[2], tok.at[4], sib)
    got("tm0", tok.at[3, half(0)])
    move("ts5", tok.at[3], tok.at[5], sib)
    wait_y(1, wo)
    make_kv(2)
    pick(2)
    wait_x1(0, wq)
    got("ts4", tok.at[4])
    got("ts5", tok.at[5])
    make_kv(4)
    pick(4)
    wait_x2(0, wq)
    wait_x1(1, wo)
    got("tf0", tok.at[6, half(0)])
    move("ts70", tok.at[6, half(0)], tok.at[7, half(0)], sib)
    got("tf1", tok.at[6, half(1)])
    move("ts71", tok.at[6, half(1)], tok.at[7, half(1)], sib)
    wait_x3(0, wq)
    got("ts70", tok.at[7, half(0)])
    got("ts71", tok.at[7, half(1)])
    make_kv(6)
    pick(6)
    wait_x2(1, wo)
    wait_s(0, wq)
    qs[...] = jnp.dot(picked[...].astype(BF16), wq[...].reshape(1024, 1024), preferred_element_type=F32).astype(BF16)
    wait_x3(1, wo)

    scale = 64 ** -0.5 * 1.4426950408889634
    lane = lax.broadcasted_iota(jnp.int32, (128, 128), 1)

    @pl.loop(0, HEADS // 2)
    def _(n):
        at = pl.ds(pl.multiple_of(n * 128, 128), 128)
        rows = qs[:, at]
        zero = jnp.zeros_like(rows)
        both = jnp.concatenate([jnp.where(lane < 64, rows, zero), jnp.where(lane >= 64, rows, zero)], axis=0)
        scores = lax.dot_general(both, kv[:, at], (((1,), (1,)), ((), ())), preferred_element_type=F32)
        peak = jnp.max(scores, axis=-1, keepdims=True)
        raw = jnp.exp2((scores - peak) * scale)
        total = jnp.sum(raw, axis=-1, keepdims=True)
        values = kv[:, pl.ds(pl.multiple_of(n * 128 + 1024, 128), 128)]
        mixed = jnp.dot(raw.astype(BF16), values, preferred_element_type=F32) / total
        att[:, at] = jnp.where(lane < 64, mixed[:128], mixed[128:]).astype(BF16)

    wait_s(1, wo)
    live = lax.broadcasted_iota(jnp.int32, (128, 1024), 0) < counts_ref[0, 0]
    result = jnp.dot(att[...], wo[...].reshape(1024, 1024), preferred_element_type=F32)
    out_ref[0, 0] = (result * jnp.where(live, 1.0, 0.0)).astype(BF16)
    for copy in started:
        copy.wait_send()


def local(frame_tokens, w_kv, w_q, w_out, slot_tokens, counts):
    hbm = pl.BlockSpec(memory_space=pl.ANY)
    vmem = pl.BlockSpec(memory_space=pltpu.VMEM)
    return pl.pallas_call(
        kernel,
        out_shape=jax.ShapeDtypeStruct((1, 1, 128, 1024), BF16),
        in_specs=[hbm, hbm, hbm, hbm, vmem, pl.BlockSpec(memory_space=pltpu.SMEM)],
        out_specs=vmem,
        scratch_shapes=[
            pltpu.VMEM((8, 128, 1024), BF16),
            pltpu.VMEM((1024, 2048), BF16),
            pltpu.VMEM((NX, 256, 1024), BF16),
            pltpu.VMEM((NX, 256, 1024), BF16),
            pltpu.VMEM((1024, 2048), BF16),
            pltpu.VMEM((128, 1024), BF16),
            pltpu.VMEM((128, 1024), BF16),
            pltpu.VMEM((128, 1024), F32),
            pltpu.SemaphoreType.DMA((len(NAMES),)),
            pltpu.SemaphoreType.DMA((len(NAMES),)),
            pltpu.SemaphoreType.DMA((4,)),
        ],
        compiler_params=pltpu.CompilerParams(
            collective_id=0, has_side_effects=True, vmem_limit_bytes=56 * 1024 * 1024
        ),
    )(frame_tokens, w_kv, w_q, w_out, slot_tokens, counts)


def solution(mesh):
    placed = (
        P("blk", "win", None, None),
        P(),
        P("win", None),
        P("win", None),
        P(None, "win", None),
        P("blk", "win"),
    )
    return jax.shard_map(
        local, mesh=mesh, in_specs=placed, out_specs=P("blk", "win", None, None), check_vma=False
    )
```

```python
import functools

import jax
import jax.numpy as jnp
from jax import lax
from jax.experimental import pallas as pl
from jax.experimental.pallas import tpu as pltpu
from jax.sharding import PartitionSpec as P

HEADS = 16
NX, NY, NZ = 4, 8, 4
MESH = pl.DeviceIdType.MESH
F32 = jnp.float32
BF16 = jnp.bfloat16

NAMES = ["own0", "own1"]
NAMES += [f"z{_k}{_s}{_h}" for _k in "pmf" for _s in range(2) for _h in range(2)]
NAMES += [f"share{_s}" for _s in range(2, 8)]
for _i in range(2):
    NAMES += [f"{_k}{_i}" for _k in ("pair", "y1p", "y1m", "y2p", "y2m", "y3p", "y3m", "y4p", "y4m")]
    NAMES += [f"x{_k}{_i}{_d}" for _k in "pmf" for _d in range(NY)]
    NAMES += [f"slab{_i}{_k}" for _k in range(NX)]
INDEX = {name: at for at, name in enumerate(NAMES)}


def kernel(tok_in, wkv_in, wq_in, wo_in, slots_ref, counts_ref, out_ref,
           tok, wkv, wq, wo, kv, qs, att, picked, send, recv, near):
    b = lax.axis_index("blk")
    w = lax.axis_index("win")
    core, zh = lax.rem(b, 2), b // 2
    zl, y, x = lax.rem(w, 2), lax.rem(w // 2, NY), w // (2 * NY)

    def at_z(d):
        return (lax.rem(zh + d, NZ) * 2, w)

    def at_xy(dx, dy, zz):
        return (b, (lax.rem(x + dx, NX) * NY + lax.rem(y + dy, NY)) * 2 + zz)

    sib = (b + 1 - 2 * core, w)
    zp, zm = at_z(1), at_z(NZ - 1)
    pair = at_xy(0, 0, 1 - zl)
    xp, xm = at_xy(1, 0, zl), at_xy(NX - 1, 0, zl)
    y1p, y1m = at_xy(0, 1, zl), at_xy(0, NY - 1, zl)
    y2p, y2m = at_xy(0, 2, zl), at_xy(0, NY - 2, zl)

    started = {0: [], 1: []}

    def descriptor(name, src, dst, device):
        return pltpu.make_async_remote_copy(
            src_ref=src, dst_ref=dst, send_sem=send.at[INDEX[name]], recv_sem=recv.at[INDEX[name]],
            device_id=device, device_id_type=MESH,
        )

    def move(who, name, src, dst, device):
        descriptor(name, src, dst, device).start()
        size = 1
        for n in dst.shape:
            size *= n
        started[who].append((name, size // 1024))

    def got(name, dst):
        descriptor(name, dst, dst, sib).wait_recv()

    def enter(devices):
        barrier = pltpu.get_barrier_semaphore()
        for device in devices:
            pl.semaphore_signal(barrier, inc=1, device_id=device, device_id_type=MESH)
        pl.semaphore_wait(barrier, len(devices))

    def sent(who):
        for name, rows in started[who]:
            part = tok.at[0, pl.ds(0, rows)] if rows <= 128 else wq.at[0, pl.ds(0, rows)]
            descriptor(name, part, part, sib).wait_send()

    load_tok = pltpu.make_async_copy(tok_in.at[0, 0], tok.at[core], near.at[0])
    load_tok.start()
    load_kv = pltpu.make_async_copy(wkv_in, wkv, near.at[1])
    load_kv.start()

    def make_kv(j):
        rows = tok[pl.ds(j, 2)].reshape(256, 1024)

        @pl.loop(0, 4)
        def _(n):
            at = pl.ds(pl.multiple_of(n * 512, 512), 512)
            kv[pl.ds(128 * j, 256), at] = jnp.dot(rows, wkv[:, at], preferred_element_type=F32).astype(BF16)

    before, after, across = lax.rem(zh + NZ - 1, NZ) * 2, lax.rem(zh + 1, NZ) * 2, lax.rem(zh + 2, NZ) * 2
    frames = [2 * zh, 2 * zh + 1, before, after, before + 1, after + 1, across, across + 1]
    wanted = slots_ref[pl.ds(b, 1), 0, :]

    def pick(j):
        hits = []
        for k in (j, j + 1):
            token = lax.broadcasted_iota(jnp.int32, (128, 128), 0) + frames[k] * 128
            hits.append(jnp.where(token == wanted, 1.0, 0.0).T.astype(BF16))
        rows = tok[pl.ds(j, 2)].reshape(256, 1024)
        part = jnp.dot(jnp.concatenate(hits, axis=1), rows, preferred_element_type=F32)
        if j == 0:
            picked[...] = part
        else:
            picked[...] += part

    def absorb(j):
        make_kv(j)
        pick(j)

    @pl.when(core == 0)
    def _():
        enter([sib, zp, zm])

        def part(slot, h):
            return tok.at[slot, pl.ds(64 * h, 64)]

        def spread(s):
            for k, h in (("p", 0), ("m", 1), ("p", 1), ("m", 0)):
                src = tok_in.at[0, 0, pl.ds(64 * h, 64)] if s == 0 else part(1, h)
                move(0, f"z{k}{s}{h}", src, part((2 if k == "p" else 3) + 2 * s, h), zp if k == "p" else zm)

        def receive(s):
            low, high = 2 + 2 * s, 3 + 2 * s
            got(f"zp{s}0", part(low, 0))
            move(0, f"zf{s}0", part(low, 0), part(6 + s, 0), zp)
            got(f"zm{s}1", part(high, 1))
            move(0, f"zf{s}1", part(high, 1), part(6 + s, 1), zm)
            got(f"zp{s}1", part(low, 1))
            move(0, f"share{low}", tok.at[low], tok.at[low], sib)
            got(f"zm{s}0", part(high, 0))
            move(0, f"share{high}", tok.at[high], tok.at[high], sib)

        spread(0)
        move(0, "own0", tok_in.at[0, 0], tok.at[0], sib)
        got("own1", tok.at[1])
        spread(1)
        load_tok.wait()
        load_kv.wait()
        absorb(0)
        receive(0)
        absorb(2)
        receive(1)
        absorb(4)
        for s in range(2):
            got(f"zf{s}0", part(6 + s, 0))
            got(f"zf{s}1", part(6 + s, 1))
            move(0, f"share{6 + s}", tok.at[6 + s], tok.at[6 + s], sib)
        absorb(6)
        for k in range(NX):
            got(f"slab0{k}", wq.at[lax.rem(x + k, NX)])

    def block(buf, k, dx=0, h=None):
        at = lax.rem(y + NY - k, NY) * 32
        if h is None:
            rows = pl.ds(pl.multiple_of(at, 32), 32)
        else:
            rows = pl.ds(pl.multiple_of(at + 16 * h, 16), 16)
        return buf.at[lax.rem(x + dx, NX), rows]

    def slab(i, buf, k):
        whole = buf.at[lax.rem(x + k, NX)]
        move(1, f"slab{i}{k}", whole, whole, sib)

    def over_x(i, buf, k):
        for name, device in (("xp", xp), ("xm", xm)):
            move(1, f"{name}{i}{k}", block(buf, k), block(buf, k), device)

    def pass_x(i, buf, k):
        got(f"xp{i}{k}", block(buf, k, NX - 1))
        if k < 4:
            move(1, f"xf{i}{k}", block(buf, k, NX - 1), block(buf, k, NX - 1), xp)
        got(f"xm{i}{k}", block(buf, k, 1))
        if k >= 4:
            move(1, f"xf{i}{k}", block(buf, k, 1), block(buf, k, 1), xm)

    def last_x(i, buf):
        for k in range(NY):
            got(f"xf{i}{k}", block(buf, k, 2))
        slab(i, buf, 2)

    both = ((0, wq), (1, wo))

    @pl.when(core == 1)
    def _():
        loads = []
        for i, src, buf in ((0, wq_in, wq), (1, wo_in, wo)):
            copy = pltpu.make_async_copy(src, block(buf, 0, 0, zl), near.at[2 + i])
            copy.start()
            loads.append(copy)
        enter([sib, pair, xp, xm, y1p, y1m, y2p, y2m])
        move(1, "pair0", wq_in, block(wq, 0, 0, zl), pair)
        move(1, "pair1", wo_in, block(wo, 0, 0, zl), pair)
        move(1, "own1", tok_in.at[0, 0], tok.at[1], sib)
        for i, buf in both:
            loads[i].wait()
            got(f"pair{i}", block(buf, 0, 0, 1 - zl))
            for name, device in (("y1p", y1p), ("y1m", y1m), ("y2p", y2p), ("y2m", y2m)):
                move(1, f"{name}{i}", block(buf, 0), block(buf, 0), device)
            over_x(i, buf, 0)
        load_tok.wait()
        load_kv.wait()
        got("own0", tok.at[0])
        absorb(0)
        for i, buf in both:
            got(f"y1p{i}", block(buf, 1))
            move(1, f"y3p{i}", block(buf, 1), block(buf, 1), y2p)
            got(f"y1m{i}", block(buf, 7))
            move(1, f"y3m{i}", block(buf, 7), block(buf, 7), y2m)
            got(f"y2p{i}", block(buf, 2))
            move(1, f"y4p{i}", block(buf, 2, 0, 0), block(buf, 2, 0, 0), y2p)
            got(f"y2m{i}", block(buf, 6))
            move(1, f"y4m{i}", block(buf, 6, 0, 1), block(buf, 6, 0, 1), y2m)
        for i, buf in both:
            for k in (1, 7, 2, 6):
                over_x(i, buf, k)
        for i, buf in both:
            pass_x(i, buf, 0)
        got("share2", tok.at[2])
        got("share3", tok.at[3])
        absorb(2)
        for i, buf in both:
            got(f"y3p{i}", block(buf, 3))
            got(f"y3m{i}", block(buf, 5))
            got(f"y4p{i}", block(buf, 4, 0, 0))
            got(f"y4m{i}", block(buf, 4, 0, 1))
            for k in (3, 5, 4):
                over_x(i, buf, k)
            slab(i, buf, 0)
        for i, buf in both:
            for k in (1, 7, 2, 6):
                pass_x(i, buf, k)
        got("share4", tok.at[4])
        got("share5", tok.at[5])
        absorb(4)
        for i, buf in both:
            for k in (3, 5, 4):
                pass_x(i, buf, k)
            slab(i, buf, 3)
            slab(i, buf, 1)
        last_x(0, wq)
        got("share6", tok.at[6])
        got("share7", tok.at[7])
        absorb(6)

    qs[...] = jnp.dot(picked[...].astype(BF16), wq[...].reshape(1024, 1024), preferred_element_type=F32).astype(BF16)

    @pl.when(core == 1)
    def _():
        last_x(1, wo)

    scale = 64 ** -0.5 * 1.4426950408889634
    lane = lax.broadcasted_iota(jnp.int32, (128, 128), 1)

    @pl.loop(0, HEADS // 2)
    def _(n):
        at = pl.ds(pl.multiple_of(n * 128, 128), 128)
        rows = qs[:, at]
        zero = jnp.zeros_like(rows)
        both = jnp.concatenate([jnp.where(lane < 64, rows, zero), jnp.where(lane >= 64, rows, zero)], axis=0)
        scores = lax.dot_general(both, kv[:, at], (((1,), (1,)), ((), ())), preferred_element_type=F32)
        peak = jnp.max(scores, axis=-1, keepdims=True)
        raw = jnp.exp2((scores - peak) * scale)
        total = jnp.sum(raw, axis=-1, keepdims=True)
        values = kv[:, pl.ds(pl.multiple_of(n * 128 + 1024, 128), 128)]
        mixed = jnp.dot(raw.astype(BF16), values, preferred_element_type=F32) / total
        att[:, at] = jnp.where(lane < 64, mixed[:128], mixed[128:]).astype(BF16)

    @pl.when(core == 0)
    def _():
        for k in range(NX):
            got(f"slab1{k}", wo.at[lax.rem(x + k, NX)])

    live = lax.broadcasted_iota(jnp.int32, (128, 1024), 0) < counts_ref[0, 0]
    result = jnp.dot(att[...], wo[...].reshape(1024, 1024), preferred_element_type=F32)
    out_ref[0, 0] = (result * jnp.where(live, 1.0, 0.0)).astype(BF16)

    for who in range(2):
        pl.when(core == who)(functools.partial(sent, who))


def local(frame_tokens, w_kv, w_q, w_out, slot_tokens, counts):
    hbm = pl.BlockSpec(memory_space=pl.ANY)
    vmem = pl.BlockSpec(memory_space=pltpu.VMEM)
    return pl.pallas_call(
        kernel,
        out_shape=jax.ShapeDtypeStruct((1, 1, 128, 1024), BF16),
        in_specs=[hbm, hbm, hbm, hbm, vmem, pl.BlockSpec(memory_space=pltpu.SMEM)],
        out_specs=vmem,
        scratch_shapes=[
            pltpu.VMEM((8, 128, 1024), BF16),
            pltpu.VMEM((1024, 2048), BF16),
            pltpu.VMEM((NX, 256, 1024), BF16),
            pltpu.VMEM((NX, 256, 1024), BF16),
            pltpu.VMEM((1024, 2048), BF16),
            pltpu.VMEM((128, 1024), BF16),
            pltpu.VMEM((128, 1024), BF16),
            pltpu.VMEM((128, 1024), F32),
            pltpu.SemaphoreType.DMA((len(NAMES),)),
            pltpu.SemaphoreType.DMA((len(NAMES),)),
            pltpu.SemaphoreType.DMA((4,)),
        ],
        compiler_params=pltpu.CompilerParams(
            collective_id=0, has_side_effects=True, vmem_limit_bytes=56 * 1024 * 1024
        ),
    )(frame_tokens, w_kv, w_q, w_out, slot_tokens, counts)


def solution(mesh):
    placed = (
        P("blk", "win", None, None),
        P(),
        P("win", None),
        P("win", None),
        P(None, "win", None),
        P("blk", "win"),
    )
    return jax.shard_map(
        local, mesh=mesh, in_specs=placed, out_specs=P("blk", "win", None, None), check_vma=False
    )
```

```python
import functools

import jax
import jax.numpy as jnp
from jax import lax
from jax.experimental import pallas as pl
from jax.experimental.pallas import tpu as pltpu
from jax.sharding import PartitionSpec as P

HEADS = 16
FRAMES = 8
NX, NY, NZ = 4, 8, 4
MESH = pl.DeviceIdType.MESH
F32 = jnp.float32
BF16 = jnp.bfloat16

NAMES = ["own0", "own1"]
NAMES += [f"z{_k}{_s}{_h}" for _k in "pmf" for _s in range(2) for _h in range(2)]
NAMES += [f"share{_s}{_h}" for _s in range(2, 8) for _h in range(2)]
NAMES += ["pair0", "pair1", "y1p", "y1m", "y2p", "y2m", "y3p", "y3m", "y4p", "y4m"]
NAMES += [f"x{_k}{_d}" for _k in "pmf" for _d in range(NY)]
NAMES += [f"slab{_k}" for _k in range(NX)]
NAMES += ["ox1", "ox2", "ox3"]
NAMES += [f"ring{_k}{_s}{_d}" for _k in "pm" for _s in range(1, 5) for _d in range(NX)]
NAMES += [f"rows{_k}" for _k in range(NY)]
INDEX = {name: at for at, name in enumerate(NAMES)}


def kernel(tok_in, wkv_in, wq_in, wo_in, slots_ref, counts_ref, out_ref,
           tok, wkv, wq, wo, kv, qs, att, picked, hits, scores, send, recv, near):
    b = lax.axis_index("blk")
    w = lax.axis_index("win")
    core, zh = lax.rem(b, 2), b // 2
    zl, y, x = lax.rem(w, 2), lax.rem(w // 2, NY), w // (2 * NY)

    def at_z(d):
        return (lax.rem(zh + d, NZ) * 2, w)

    def at_xy(dx, dy, zz):
        return (b, (lax.rem(x + dx, NX) * NY + lax.rem(y + dy, NY)) * 2 + zz)

    sib = (b + 1 - 2 * core, w)
    zp, zm = at_z(1), at_z(NZ - 1)
    pair = at_xy(0, 0, 1 - zl)
    xp, xm, x2 = at_xy(1, 0, zl), at_xy(NX - 1, 0, zl), at_xy(2, 0, zl)
    y1p, y1m = at_xy(0, 1, zl), at_xy(0, NY - 1, zl)
    y2p, y2m = at_xy(0, 2, zl), at_xy(0, NY - 2, zl)

    started = {0: [], 1: []}

    def descriptor(name, src, dst, device):
        return pltpu.make_async_remote_copy(
            src_ref=src, dst_ref=dst, send_sem=send.at[INDEX[name]], recv_sem=recv.at[INDEX[name]],
            device_id=device, device_id_type=MESH,
        )

    def move(who, name, src, dst, device):
        descriptor(name, src, dst, device).start()
        size = 1
        for n in dst.shape:
            size *= n
        started[who].append((name, size // 1024))

    def got(name, dst):
        descriptor(name, dst, dst, sib).wait_recv()

    def enter(devices):
        barrier = pltpu.get_barrier_semaphore()
        for device in devices:
            pl.semaphore_signal(barrier, inc=1, device_id=device, device_id_type=MESH)
        pl.semaphore_wait(barrier, len(devices))

    def sent(who):
        for name, rows in started[who]:
            part = tok.at[0, pl.ds(0, rows)] if rows <= 128 else wq.at[0, pl.ds(0, rows)]
            descriptor(name, part, part, sib).wait_send()

    load_tok = pltpu.make_async_copy(tok_in.at[0, 0], tok.at[core], near.at[0])
    load_tok.start()
    load_kv = pltpu.make_async_copy(wkv_in, wkv, near.at[1])
    load_kv.start()

    before, after, across = lax.rem(zh + NZ - 1, NZ) * 2, lax.rem(zh + 1, NZ) * 2, lax.rem(zh + 2, NZ) * 2
    frames = [2 * zh, 2 * zh + 1, before, after, before + 1, after + 1, across, across + 1]
    wanted = slots_ref[pl.ds(b, 1), 0, :]

    def part(slot, h):
        return tok.at[slot, pl.ds(64 * h, 64)]

    def spread(s):
        for k, h in (("p", 0), ("m", 1), ("p", 1), ("m", 0)):
            src = tok_in.at[0, 0, pl.ds(64 * h, 64)] if s == 0 else part(1, h)
            move(0, f"z{k}{s}{h}", src, part((2 if k == "p" else 3) + 2 * s, h), zp if k == "p" else zm)

    def share(slot, h):
        move(0, f"share{slot}{h}", part(slot, h), part(slot, h), sib)

    def z_pass(s):
        low, high = 2 + 2 * s, 3 + 2 * s
        got(f"zp{s}0", part(low, 0))
        move(0, f"zf{s}0", part(low, 0), part(6 + s, 0), zp)
        got(f"zm{s}1", part(high, 1))
        move(0, f"zf{s}1", part(high, 1), part(6 + s, 1), zm)
        share(low, 0)
        share(high, 1)

    def z_near(s):
        low, high = 2 + 2 * s, 3 + 2 * s
        got(f"zp{s}1", part(low, 1))
        share(low, 1)
        got(f"zm{s}0", part(high, 0))
        share(high, 0)

    def z_far(s):
        got(f"zf{s}0", part(6 + s, 0))
        share(6 + s, 0)
        got(f"zf{s}1", part(6 + s, 1))
        share(6 + s, 1)

    def shared(*slots):
        for slot in slots:
            for h in range(2):
                got(f"share{slot}{h}", part(slot, h))

    def block(buf, k, dx=0, h=None):
        at = lax.rem(y + NY - k, NY) * 32
        if h is None:
            rows = pl.ds(pl.multiple_of(at, 32), 32)
        else:
            rows = pl.ds(pl.multiple_of(at + 16 * h, 16), 16)
        return buf.at[lax.rem(x + dx, NX), rows]

    def slab(k):
        whole = wq.at[lax.rem(x + k, NX)]
        move(1, f"slab{k}", whole, whole, sib)

    def over_x(*ks):
        for k in ks:
            for name, device in (("xp", xp), ("xm", xm)):
                move(1, f"{name}{k}", block(wq, k), block(wq, k), device)

    def pass_x(*ks):
        for k in ks:
            got(f"xp{k}", block(wq, k, NX - 1))
            if k < 4:
                move(1, f"xf{k}", block(wq, k, NX - 1), block(wq, k, NX - 1), xp)
            got(f"xm{k}", block(wq, k, 1))
            if k >= 4:
                move(1, f"xf{k}", block(wq, k, 1), block(wq, k, 1), xm)

    def last_x():
        for k in range(NY):
            got(f"xf{k}", block(wq, k, 2))
        slab(2)

    def y_first():
        for name, device in (("y1p", y1p), ("y1m", y1m), ("y2p", y2p), ("y2m", y2m)):
            move(1, name, block(wq, 0), block(wq, 0), device)

    def y_pass():
        got("y1p", block(wq, 1))
        move(1, "y3p", block(wq, 1), block(wq, 1), y2p)
        got("y1m", block(wq, 7))
        move(1, "y3m", block(wq, 7), block(wq, 7), y2m)
        got("y2p", block(wq, 2))
        move(1, "y4p", block(wq, 2, 0, 0), block(wq, 2, 0, 0), y2p)
        got("y2m", block(wq, 6))
        move(1, "y4m", block(wq, 6, 0, 1), block(wq, 6, 0, 1), y2m)

    def y_last():
        got("y3p", block(wq, 3))
        got("y3m", block(wq, 5))
        got("y4p", block(wq, 4, 0, 0))
        got("y4m", block(wq, 4, 0, 1))

    def ring(step, dx):
        if step < 4 or dx < 2:
            up = block(wo, step - 1, dx)
            move(1, f"ringp{step}{dx}", up, up, y1p)
        if step < 4 or dx >= 2:
            down = block(wo, (NY + 1 - step) % NY, dx)
            move(1, f"ringm{step}{dx}", down, down, y1m)

    def came(step, dx):
        if step < 4 or dx < 2:
            got(f"ringp{step}{dx}", block(wo, step, dx))
        if step < 4 or dx >= 2:
            got(f"ringm{step}{dx}", block(wo, NY - step, dx))

    def ring_pass(step, *dxs):
        for dx in dxs:
            came(step, dx)
            ring(step + 1, dx)

    def rows_of(k):
        at = pl.multiple_of(lax.rem(y + NY - k, NY) * 32, 32)
        return wo.at[:, pl.ds(at, 32)]

    def rows(*ks):
        for k in ks:
            move(1, f"rows{k}", rows_of(k), rows_of(k), sib)

    @pl.when(core == 0)
    def _():
        enter([sib, zp, zm])
        spread(0)
        move(0, "own0", tok_in.at[0, 0], tok.at[0], sib)

    @pl.when(core == 1)
    def _():
        loads = []
        for i, src, buf in ((0, wq_in, wq), (1, wo_in, wo)):
            copy = pltpu.make_async_copy(src, block(buf, 0, 0, zl), near.at[2 + i])
            copy.start()
            loads.append(copy)
        enter([sib, pair, xp, xm, x2, y1p, y1m, y2p, y2m])
        move(1, "own1", tok_in.at[0, 0], tok.at[1], sib)
        move(1, "pair0", wq_in, block(wq, 0, 0, zl), pair)
        move(1, "pair1", wo_in, block(wo, 0, 0, zl), pair)
        for copy in loads:
            copy.wait()

    for j in range(FRAMES):
        token = lax.broadcasted_iota(jnp.int32, (128, 128), 0) + frames[j] * 128
        hits[:, 128 * j:128 * j + 128] = jnp.where(token == wanted, 1.0, 0.0).T.astype(BF16)
    picked[...] = jnp.zeros_like(picked)

    @pl.when(core == 0)
    def _():
        got("own1", tok.at[1])
        spread(1)

    @pl.when(core == 1)
    def _():
        got("pair0", block(wq, 0, 0, 1 - zl))
        y_first()
        over_x(0)
        got("pair1", block(wo, 0, 0, 1 - zl))
        for dx, device in ((1, xp), (3, xm), (2, x2)):
            move(1, f"ox{dx}", block(wo, 0), block(wo, 0), device)
        ring(1, 0)
        got("own0", tok.at[0])

    load_tok.wait()
    load_kv.wait()

    def from_x():
        for dx in (1, 3, 2):
            got(f"ox{dx}", block(wo, 0, (NX - dx) % NX))
            ring(1, (NX - dx) % NX)

    def ring_end():
        for dx in range(NX):
            came(4, dx)

    near_order = (0, 3, 1, 2)
    events = {
        (0, 2): [(z_pass, 0), (z_near, 0)],
        (0, 4): [(z_pass, 1), (z_near, 1)],
        (0, 6): [(z_far, 0)],
        (0, 7): [(z_far, 1)],
        (1, 2): [(y_pass,), (over_x, 1, 7, 2, 6), (from_x,), (rows, 0), (pass_x, 0), (ring_pass, 1) + near_order, (shared, 2)],
        (1, 3): [(y_last,), (over_x, 3, 5, 4), (slab, 0), (shared, 3)],
        (1, 4): [(ring_pass, 2) + near_order, (rows, 1, 7), (pass_x, 1, 7, 2, 6), (ring_pass, 3) + near_order,
                 (rows, 2, 6), (shared, 4)],
        (1, 5): [(pass_x, 3, 5, 4), (slab, 3), (slab, 1), (rows, 3, 5), (shared, 5)],
        (1, 6): [(ring_end,), (rows, 4), (last_x,), (shared, 6)],
        (1, 7): [(shared, 7)],
    }

    @pl.loop(0, FRAMES)
    def _(t):
        for (who, when), calls in events.items():
            @pl.when((core == who) & (t == when))
            def _(calls=calls):
                for call in calls:
                    call[0](*call[1:])

        at = pl.ds(pl.multiple_of(t * 128, 128), 128)
        kv[at, :] = jnp.dot(tok[t], wkv[...], preferred_element_type=F32).astype(BF16)
        picked[...] += jnp.dot(hits[:, at], tok[t], preferred_element_type=F32)

    @pl.when(core == 0)
    def _():
        for k in range(NX):
            got(f"slab{k}", wq.at[lax.rem(x + k, NX)])

    qs[...] = jnp.dot(picked[...].astype(BF16), wq[...].reshape(1024, 1024), preferred_element_type=F32).astype(BF16)

    scale = 64 ** -0.5 * 1.4426950408889634
    lane = lax.broadcasted_iota(jnp.int32, (128, 256), 1)

    def head(h):
        return (lane >= 64 * h) & (lane < 64 * h + 64)

    def score(n):
        rows = qs[:, 256 * n:256 * n + 256]
        zero = jnp.zeros_like(rows)
        stack = jnp.concatenate([jnp.where(head(h), rows, zero) for h in range(4)], axis=0)
        keys = kv[:, 256 * n:256 * n + 256]
        return lax.dot_general(stack, keys, (((1,), (1,)), ((), ())), preferred_element_type=F32)

    groups = HEADS // 4
    scores[0] = score(0)
    for n in range(groups):
        later = score(n + 1) if n + 1 < groups else None
        now = scores[n % 2]
        peak = jnp.max(now, axis=-1, keepdims=True)
        raw = jnp.exp2((now - peak) * scale)
        total = jnp.sum(raw, axis=-1, keepdims=True)
        values = kv[:, 1024 + 256 * n:1280 + 256 * n]
        mixed = jnp.dot(raw.astype(BF16), values, preferred_element_type=F32) / total
        result = mixed[384:]
        for h in range(3):
            result = jnp.where(head(h), mixed[128 * h:128 * h + 128], result)
        att[:, 256 * n:256 * n + 256] = result.astype(BF16)
        if later is not None:
            scores[(n + 1) % 2] = later

    @pl.when(core == 0)
    def _():
        for k in range(NY):
            got(f"rows{k}", rows_of(k))

    live = lax.broadcasted_iota(jnp.int32, (128, 1024), 0) < counts_ref[0, 0]
    result = jnp.dot(att[...], wo[...].reshape(1024, 1024), preferred_element_type=F32)
    out_ref[0, 0] = (result * jnp.where(live, 1.0, 0.0)).astype(BF16)

    for who in range(2):
        pl.when(core == who)(functools.partial(sent, who))


def local(frame_tokens, w_kv, w_q, w_out, slot_tokens, counts):
    hbm = pl.BlockSpec(memory_space=pl.ANY)
    vmem = pl.BlockSpec(memory_space=pltpu.VMEM)
    return pl.pallas_call(
        kernel,
        out_shape=jax.ShapeDtypeStruct((1, 1, 128, 1024), BF16),
        in_specs=[hbm, hbm, hbm, hbm, vmem, pl.BlockSpec(memory_space=pltpu.SMEM)],
        out_specs=vmem,
        scratch_shapes=[
            pltpu.VMEM((8, 128, 1024), BF16),
            pltpu.VMEM((1024, 2048), BF16),
            pltpu.VMEM((NX, 256, 1024), BF16),
            pltpu.VMEM((NX, 256, 1024), BF16),
            pltpu.VMEM((1024, 2048), BF16),
            pltpu.VMEM((128, 1024), BF16),
            pltpu.VMEM((128, 1024), BF16),
            pltpu.VMEM((128, 1024), F32),
            pltpu.VMEM((128, 1024), BF16),
            pltpu.VMEM((2, 512, 1024), F32),
            pltpu.SemaphoreType.DMA((len(NAMES),)),
            pltpu.SemaphoreType.DMA((len(NAMES),)),
            pltpu.SemaphoreType.DMA((4,)),
        ],
        compiler_params=pltpu.CompilerParams(
            collective_id=0, has_side_effects=True, vmem_limit_bytes=56 * 1024 * 1024
        ),
    )(frame_tokens, w_kv, w_q, w_out, slot_tokens, counts)


def solution(mesh):
    placed = (
        P("blk", "win", None, None),
        P(),
        P("win", None),
        P("win", None),
        P(None, "win", None),
        P("blk", "win"),
    )
    return jax.shard_map(
        local, mesh=mesh, in_specs=placed, out_specs=P("blk", "win", None, None), check_vma=False
    )
```

```python
import functools

import jax
import jax.numpy as jnp
from jax import lax
from jax.experimental import pallas as pl
from jax.experimental.pallas import tpu as pltpu
from jax.sharding import PartitionSpec as P

HEADS = 16
FRAMES = 8
NX, NY, NZ = 4, 8, 4
MESH = pl.DeviceIdType.MESH
F32 = jnp.float32
BF16 = jnp.bfloat16

NAMES = ["own0", "own1"]
NAMES += [f"z{_k}{_s}{_h}" for _k in "pmf" for _s in range(2) for _h in range(2)]
NAMES += [f"share{_s}{_h}" for _s in range(2, 8) for _h in range(2)]
NAMES += ["pair0", "pair1", "y1p", "y1m", "y2p", "y2m", "y3p", "y3m", "y4p", "y4m"]
NAMES += [f"x{_k}{_d}" for _k in "pmf" for _d in range(NY)]
NAMES += [f"slab{_k}" for _k in range(NX)]
NAMES += ["ox1", "ox2", "ox3"]
NAMES += [f"ring{_k}{_s}{_d}" for _k in "pm" for _s in range(1, 5) for _d in range(NX)]
NAMES += [f"rows{_k}" for _k in range(NY)]
INDEX = {name: at for at, name in enumerate(NAMES)}


def kernel(tok_in, wkv_in, wq_in, wo_in, slots_ref, counts_ref, out_ref,
           tok, wkv, wq, wo, kv, qs, att, picked, hits, scores, send, recv, near, hello):
    b = lax.axis_index("blk")
    w = lax.axis_index("win")
    core, zh = lax.rem(b, 2), b // 2
    zl, y, x = lax.rem(w, 2), lax.rem(w // 2, NY), w // (2 * NY)

    def at_z(d):
        return (lax.rem(zh + d, NZ) * 2, w)

    def at_xy(dx, dy, zz):
        return (b, (lax.rem(x + dx, NX) * NY + lax.rem(y + dy, NY)) * 2 + zz)

    sib = (b + 1 - 2 * core, w)
    zp, zm = at_z(1), at_z(NZ - 1)
    pair = at_xy(0, 0, 1 - zl)
    xp, xm, x2 = at_xy(1, 0, zl), at_xy(NX - 1, 0, zl), at_xy(2, 0, zl)
    y1p, y1m = at_xy(0, 1, zl), at_xy(0, NY - 1, zl)
    y2p, y2m = at_xy(0, 2, zl), at_xy(0, NY - 2, zl)

    started = {0: [], 1: []}

    def descriptor(name, src, dst, device):
        return pltpu.make_async_remote_copy(
            src_ref=src, dst_ref=dst, send_sem=send.at[INDEX[name]], recv_sem=recv.at[INDEX[name]],
            device_id=device, device_id_type=MESH,
        )

    def move(who, name, src, dst, device):
        descriptor(name, src, dst, device).start()
        size = 1
        for n in dst.shape:
            size *= n
        if (name, size // 1024) not in started[who]:
            started[who].append((name, size // 1024))

    def got(name, dst):
        descriptor(name, dst, dst, sib).wait_recv()

    def announce(devices):
        barrier = pltpu.get_barrier_semaphore()
        for device in devices:
            pl.semaphore_signal(barrier, inc=1, device_id=device, device_id_type=MESH)

    def arrive(count):
        pl.semaphore_wait(pltpu.get_barrier_semaphore(), count)

    def sent(who):
        for name, rows in started[who]:
            part = tok.at[0, pl.ds(0, rows)] if rows <= 128 else wq.at[0, pl.ds(0, rows)]
            descriptor(name, part, part, sib).wait_send()

    load_tok = pltpu.make_async_copy(tok_in.at[0, 0], tok.at[core], near.at[0])
    load_tok.start()
    load_kv = pltpu.make_async_copy(wkv_in, wkv, near.at[1])
    load_kv.start()

    before, after, across = lax.rem(zh + NZ - 1, NZ) * 2, lax.rem(zh + 1, NZ) * 2, lax.rem(zh + 2, NZ) * 2
    frames = [2 * zh, 2 * zh + 1, before, after, before + 1, after + 1, across, across + 1]
    wanted = slots_ref[pl.ds(b, 1), 0, :]

    def part(slot, h):
        return tok.at[slot, pl.ds(64 * h, 64)]

    def spread(s):
        for k, h in (("p", 0), ("m", 1), ("p", 1), ("m", 0)):
            src = tok_in.at[0, 0, pl.ds(64 * h, 64)] if s == 0 else part(1, h)
            move(0, f"z{k}{s}{h}", src, part((2 if k == "p" else 3) + 2 * s, h), zp if k == "p" else zm)

    def share(slot, h):
        move(0, f"share{slot}{h}", part(slot, h), part(slot, h), sib)

    def z_pass(s):
        low, high = 2 + 2 * s, 3 + 2 * s
        got(f"zp{s}0", part(low, 0))
        move(0, f"zf{s}0", part(low, 0), part(6 + s, 0), zp)
        got(f"zm{s}1", part(high, 1))
        move(0, f"zf{s}1", part(high, 1), part(6 + s, 1), zm)
        share(low, 0)
        share(high, 1)

    def z_near(s):
        low, high = 2 + 2 * s, 3 + 2 * s
        got(f"zp{s}1", part(low, 1))
        share(low, 1)
        got(f"zm{s}0", part(high, 0))
        share(high, 0)

    def z_far(s):
        got(f"zf{s}0", part(6 + s, 0))
        share(6 + s, 0)
        got(f"zf{s}1", part(6 + s, 1))
        share(6 + s, 1)

    def shared(*slots):
        for slot in slots:
            for h in range(2):
                got(f"share{slot}{h}", part(slot, h))

    def block(buf, k, dx=0, h=None):
        at = lax.rem(y + NY - k, NY) * 32
        if h is None:
            rows = pl.ds(pl.multiple_of(at, 32), 32)
        else:
            rows = pl.ds(pl.multiple_of(at + 16 * h, 16), 16)
        return buf.at[lax.rem(x + dx, NX), rows]

    def slab(k):
        whole = wq.at[lax.rem(x + k, NX)]
        move(1, f"slab{k}", whole, whole, sib)

    def over_x(*ks):
        for k in ks:
            for name, device in (("xp", xp), ("xm", xm)):
                move(1, f"{name}{k}", block(wq, k), block(wq, k), device)

    def pass_x(*ks):
        for k in ks:
            got(f"xp{k}", block(wq, k, NX - 1))
            if k < 4:
                move(1, f"xf{k}", block(wq, k, NX - 1), block(wq, k, NX - 1), xp)
            got(f"xm{k}", block(wq, k, 1))
            if k >= 4:
                move(1, f"xf{k}", block(wq, k, 1), block(wq, k, 1), xm)

    def last_x():
        for k in range(NY):
            got(f"xf{k}", block(wq, k, 2))
        slab(2)

    def y_first():
        for name, device in (("y1p", y1p), ("y1m", y1m), ("y2p", y2p), ("y2m", y2m)):
            move(1, name, block(wq, 0), block(wq, 0), device)

    def y_pass():
        got("y1p", block(wq, 1))
        move(1, "y3p", block(wq, 1), block(wq, 1), y2p)
        got("y1m", block(wq, 7))
        move(1, "y3m", block(wq, 7), block(wq, 7), y2m)
        got("y2p", block(wq, 2))
        move(1, "y4p", block(wq, 2, 0, 0), block(wq, 2, 0, 0), y2p)
        got("y2m", block(wq, 6))
        move(1, "y4m", block(wq, 6, 0, 1), block(wq, 6, 0, 1), y2m)

    def y_last():
        got("y3p", block(wq, 3))
        got("y3m", block(wq, 5))
        got("y4p", block(wq, 4, 0, 0))
        got("y4m", block(wq, 4, 0, 1))

    def ring(step, dx):
        if step < 4 or dx < 2:
            up = block(wo, step - 1, dx)
            move(1, f"ringp{step}{dx}", up, up, y1p)
        if step < 4 or dx >= 2:
            down = block(wo, (NY + 1 - step) % NY, dx)
            move(1, f"ringm{step}{dx}", down, down, y1m)

    def came(step, dx):
        if step < 4 or dx < 2:
            got(f"ringp{step}{dx}", block(wo, step, dx))
        if step < 4 or dx >= 2:
            got(f"ringm{step}{dx}", block(wo, NY - step, dx))

    def ring_pass(step, *dxs):
        for dx in dxs:
            came(step, dx)
            ring(step + 1, dx)

    def rows_of(k):
        at = pl.multiple_of(lax.rem(y + NY - k, NY) * 32, 32)
        return wo.at[:, pl.ds(at, 32)]

    def rows(*ks):
        for k in ks:
            move(1, f"rows{k}", rows_of(k), rows_of(k), sib)

    def give_own():
        pl.semaphore_wait(hello, 1)
        descriptor("own1", tok_in.at[0, 0], tok.at[1], sib).start()

    started[1].append(("own1", 128))

    @pl.when(core == 0)
    def _():
        announce([zp, zm])
        arrive(3)
        pl.semaphore_signal(hello, inc=1, device_id=sib, device_id_type=MESH)
        spread(0)
        move(0, "own0", tok_in.at[0, 0], tok.at[0], sib)

    @pl.when(core == 1)
    def _():
        loads = []
        for i, src, buf in ((0, wq_in, wq), (1, wo_in, wo)):
            copy = pltpu.make_async_copy(src, block(buf, 0, 0, zl), near.at[2 + i])
            copy.start()
            loads.append(copy)
        across_xy = [pair, xp, xm, x2, y1p, y1m, y2p, y2m]
        announce([sib] + across_xy)
        pl.when(zh >= NZ // 2)(give_own)
        arrive(len(across_xy))
        move(1, "pair0", wq_in, block(wq, 0, 0, zl), pair)
        move(1, "pair1", wo_in, block(wo, 0, 0, zl), pair)
        for copy in loads:
            copy.wait()

    for j in range(FRAMES):
        token = lax.broadcasted_iota(jnp.int32, (128, 128), 0) + frames[j] * 128
        hits[:, 128 * j:128 * j + 128] = jnp.where(token == wanted, 1.0, 0.0).T.astype(BF16)
    picked[...] = jnp.zeros_like(picked)

    @pl.when(core == 0)
    def _():
        got("own1", tok.at[1])
        spread(1)

    @pl.when(core == 1)
    def _():
        got("pair0", block(wq, 0, 0, 1 - zl))
        y_first()
        over_x(0)
        got("pair1", block(wo, 0, 0, 1 - zl))
        for dx, device in ((1, xp), (3, xm), (2, x2)):
            move(1, f"ox{dx}", block(wo, 0), block(wo, 0), device)
        ring(1, 0)
        pl.when(zh < NZ // 2)(give_own)
        got("own0", tok.at[0])

    load_tok.wait()
    load_kv.wait()

    def from_x():
        for dx in (1, 3, 2):
            got(f"ox{dx}", block(wo, 0, (NX - dx) % NX))
            ring(1, (NX - dx) % NX)

    def ring_end():
        for dx in range(NX):
            came(4, dx)

    near_order = (0, 3, 1, 2)
    early, late = zh < NZ // 2, zh >= NZ // 2
    first = core == 0
    by_y = [(y_pass,), (over_x, 1, 7, 2, 6), (from_x,), (rows, 0), (pass_x, 0), (ring_pass, 1) + near_order]
    by_y_end = [(y_last,), (over_x, 3, 5, 4), (slab, 0)]
    middle = [(ring_pass, 2) + near_order, (rows, 1, 7), (pass_x, 1, 7, 2, 6), (ring_pass, 3) + near_order, (rows, 2, 6)]
    by_x_end = [(pass_x, 3, 5, 4), (slab, 3), (slab, 1), (rows, 3, 5)]
    finish = [(ring_end,), (rows, 4), (last_x,)]
    events = [
        (first, 2, [(z_pass, 0), (z_near, 0)]),
        (first, 4, [(z_pass, 1), (z_near, 1)]),
        (first, 6, [(z_far, 0)]),
        (first, 7, [(z_far, 1)]),
        (~first, 2, by_y),
        (~first & early, 2, by_y_end + [(ring_pass, 2) + near_order, (rows, 1, 7)]),
        (~first, 2, [(shared, 2)]),
        (~first & late, 3, by_y_end),
        (~first & early, 3, [(pass_x, 1, 7, 2, 6)]),
        (~first, 3, [(shared, 3)]),
        (~first & late, 4, middle),
        (~first & early, 4, [(ring_pass, 3) + near_order, (rows, 2, 6)] + by_x_end),
        (~first, 4, [(shared, 4)]),
        (~first & late, 5, by_x_end),
        (~first, 5, [(shared, 5)]),
        (~first, 6, finish + [(shared, 6)]),
        (~first, 7, [(shared, 7)]),
    ]

    @pl.loop(0, FRAMES)
    def _(t):
        for who, when, calls in events:
            @pl.when(who & (t == when))
            def _(calls=calls):
                for call in calls:
                    call[0](*call[1:])

        at = pl.ds(pl.multiple_of(t * 128, 128), 128)
        kv[at, :] = jnp.dot(tok[t], wkv[...], preferred_element_type=F32).astype(BF16)
        picked[...] += jnp.dot(hits[:, at], tok[t], preferred_element_type=F32)

    @pl.when(core == 0)
    def _():
        for k in range(NX):
            got(f"slab{k}", wq.at[lax.rem(x + k, NX)])

    qs[...] = jnp.dot(picked[...].astype(BF16), wq[...].reshape(1024, 1024), preferred_element_type=F32).astype(BF16)

    scale = 64 ** -0.5 * 1.4426950408889634
    lane = lax.broadcasted_iota(jnp.int32, (128, 256), 1)

    def head(h):
        return (lane >= 64 * h) & (lane < 64 * h + 64)

    def score(n):
        rows = qs[:, 256 * n:256 * n + 256]
        zero = jnp.zeros_like(rows)
        stack = jnp.concatenate([jnp.where(head(h), rows, zero) for h in range(4)], axis=0)
        keys = kv[:, 256 * n:256 * n + 256]
        return lax.dot_general(stack, keys, (((1,), (1,)), ((), ())), preferred_element_type=F32)

    groups = HEADS // 4
    scores[0] = score(0)
    for n in range(groups):
        later = score(n + 1) if n + 1 < groups else None
        now = scores[n % 2]
        peak = jnp.max(now, axis=-1, keepdims=True)
        raw = jnp.exp2((now - peak) * scale)
        total = jnp.sum(raw, axis=-1, keepdims=True)
        values = kv[:, 1024 + 256 * n:1280 + 256 * n]
        mixed = jnp.dot(raw.astype(BF16), values, preferred_element_type=F32) / total
        result = mixed[384:]
        for h in range(3):
            result = jnp.where(head(h), mixed[128 * h:128 * h + 128], result)
        att[:, 256 * n:256 * n + 256] = result.astype(BF16)
        if later is not None:
            scores[(n + 1) % 2] = later

    @pl.when(core == 0)
    def _():
        for k in range(NY):
            got(f"rows{k}", rows_of(k))

    live = lax.broadcasted_iota(jnp.int32, (128, 1024), 0) < counts_ref[0, 0]
    result = jnp.dot(att[...], wo[...].reshape(1024, 1024), preferred_element_type=F32)
    out_ref[0, 0] = (result * jnp.where(live, 1.0, 0.0)).astype(BF16)

    for who in range(2):
        pl.when(core == who)(functools.partial(sent, who))


def local(frame_tokens, w_kv, w_q, w_out, slot_tokens, counts):
    hbm = pl.BlockSpec(memory_space=pl.ANY)
    vmem = pl.BlockSpec(memory_space=pltpu.VMEM)
    return pl.pallas_call(
        kernel,
        out_shape=jax.ShapeDtypeStruct((1, 1, 128, 1024), BF16),
        in_specs=[hbm, hbm, hbm, hbm, vmem, pl.BlockSpec(memory_space=pltpu.SMEM)],
        out_specs=vmem,
        scratch_shapes=[
            pltpu.VMEM((8, 128, 1024), BF16),
            pltpu.VMEM((1024, 2048), BF16),
            pltpu.VMEM((NX, 256, 1024), BF16),
            pltpu.VMEM((NX, 256, 1024), BF16),
            pltpu.VMEM((1024, 2048), BF16),
            pltpu.VMEM((128, 1024), BF16),
            pltpu.VMEM((128, 1024), BF16),
            pltpu.VMEM((128, 1024), F32),
            pltpu.VMEM((128, 1024), BF16),
            pltpu.VMEM((2, 512, 1024), F32),
            pltpu.SemaphoreType.DMA((len(NAMES),)),
            pltpu.SemaphoreType.DMA((len(NAMES),)),
            pltpu.SemaphoreType.DMA((4,)),
            pltpu.SemaphoreType.REGULAR,
        ],
        compiler_params=pltpu.CompilerParams(
            collective_id=0, has_side_effects=True, vmem_limit_bytes=56 * 1024 * 1024
        ),
    )(frame_tokens, w_kv, w_q, w_out, slot_tokens, counts)


def solution(mesh):
    placed = (
        P("blk", "win", None, None),
        P(),
        P("win", None),
        P("win", None),
        P(None, "win", None),
        P("blk", "win"),
    )
    return jax.shard_map(
        local, mesh=mesh, in_specs=placed, out_specs=P("blk", "win", None, None), check_vma=False
    )
```

```python
import functools

import jax
import jax.numpy as jnp
from jax import lax
from jax.experimental import pallas as pl
from jax.experimental.pallas import tpu as pltpu
from jax.sharding import PartitionSpec as P

HEADS = 16
FRAMES = 8
NX, NY, NZ = 4, 8, 4
MESH = pl.DeviceIdType.MESH
F32 = jnp.float32
BF16 = jnp.bfloat16

NAMES = ["own0", "own1"]
NAMES += [f"z{_k}{_s}{_h}" for _k in "pmf" for _s in range(2) for _h in range(2)]
NAMES += [f"share{_s}{_h}" for _s in range(2, 8) for _h in range(2)]
NAMES += ["pair0", "pair1", "y1p", "y1m", "y2p", "y2m", "y3p", "y3m", "y4p", "y4m"]
NAMES += [f"x{_k}{_d}" for _k in "pmf" for _d in range(NY)]
NAMES += [f"slab{_k}" for _k in range(NX)]
NAMES += ["ox1", "ox2", "ox3"]
NAMES += [f"ring{_k}{_s}{_d}" for _k in "pm" for _s in range(1, 5) for _d in range(NX)]
NAMES += [f"rows{_k}" for _k in range(NY)]
KINDS = ("own", "z", "share", "pair", "y", "x", "slab", "ox", "ring", "rows")


def kind_of(name):
    for kind in sorted(KINDS, key=len, reverse=True):
        if name.startswith(kind):
            return KINDS.index(kind)


INDEX = {}
for _name in NAMES:
    _key = _name[:2] if _name[:2] == "xf" else _name[:4] if _name[:4] in ("rows", "slab") else _name
    INDEX[_name] = INDEX.setdefault(_key, len(set(INDEX.values())))
SLOTS = max(INDEX.values()) + 1


def kernel(tok_in, wkv_in, wq_in, wo_in, slots_ref, counts_ref, out_ref,
           tok, wkv, wq, wo, kv, qs, att, picked, hits, scores, send, recv, near, hello):
    b = lax.axis_index("blk")
    w = lax.axis_index("win")
    core, zh = lax.rem(b, 2), b // 2
    zl, y, x = lax.rem(w, 2), lax.rem(w // 2, NY), w // (2 * NY)

    def at_z(d):
        return (lax.rem(zh + d, NZ) * 2, w)

    def at_xy(dx, dy, zz):
        return (b, (lax.rem(x + dx, NX) * NY + lax.rem(y + dy, NY)) * 2 + zz)

    sib = (b + 1 - 2 * core, w)
    zp, zm = at_z(1), at_z(NZ - 1)
    pair = at_xy(0, 0, 1 - zl)
    xp, xm, x2 = at_xy(1, 0, zl), at_xy(NX - 1, 0, zl), at_xy(2, 0, zl)
    y1p, y1m = at_xy(0, 1, zl), at_xy(0, NY - 1, zl)
    y2p, y2m = at_xy(0, 2, zl), at_xy(0, NY - 2, zl)

    def descriptor(name, src, dst, device):
        return pltpu.make_async_remote_copy(
            src_ref=src, dst_ref=dst, send_sem=send.at[kind_of(name)], recv_sem=recv.at[INDEX[name]],
            device_id=device, device_id_type=MESH,
        )

    def move(who, name, src, dst, device):
        descriptor(name, src, dst, device).start()

    def got(name, dst):
        descriptor(name, dst, dst, sib).wait_recv()

    def announce(devices):
        barrier = pltpu.get_barrier_semaphore()
        for device in devices:
            pl.semaphore_signal(barrier, inc=1, device_id=device, device_id_type=MESH)

    def arrive(count):
        pl.semaphore_wait(pltpu.get_barrier_semaphore(), count)

    def sent(who):
        kinds = (("own0", tok.at[0]), ("zp00", tok.at[pl.ds(0, 6)]), ("share20", tok.at[pl.ds(0, 6)])) if who == 0 else (
            ("own1", tok.at[0]), ("pair0", wq.at[0, pl.ds(0, 32)]), ("y1p", wq.at[0, pl.ds(0, 224)]),
            ("xp0", wq.at[pl.ds(0, 3)]), ("slab0", wq), ("ox1", wq.at[0, pl.ds(0, 96)]),
            ("ringp10", tok.at[pl.ds(0, 7)]), ("rows0", wo))
        for name, part in kinds:
            descriptor(name, part, part, sib).wait_send()

    across_xy = [pair, xp, xm, x2, y1p, y1m, y2p, y2m]
    pl.when(core == 0)(lambda: announce([zp, zm]))
    pl.when(core == 1)(lambda: announce([sib] + across_xy))

    load_tok = pltpu.make_async_copy(tok_in.at[0, 0], tok.at[core], near.at[0])
    load_tok.start()
    load_kv = pltpu.make_async_copy(wkv_in, wkv, near.at[1])
    load_kv.start()

    before, after, across = lax.rem(zh + NZ - 1, NZ) * 2, lax.rem(zh + 1, NZ) * 2, lax.rem(zh + 2, NZ) * 2
    frames = [2 * zh, 2 * zh + 1, before, after, before + 1, after + 1, across, across + 1]
    wanted = slots_ref[pl.ds(b, 1), 0, :]

    def part(slot, h):
        return tok.at[slot, pl.ds(64 * h, 64)]

    def spread(s):
        for k, h in (("p", 0), ("m", 1), ("p", 1), ("m", 0)):
            src = tok_in.at[0, 0, pl.ds(64 * h, 64)] if s == 0 else part(1, h)
            move(0, f"z{k}{s}{h}", src, part((2 if k == "p" else 3) + 2 * s, h), zp if k == "p" else zm)

    def share(slot, h):
        move(0, f"share{slot}{h}", part(slot, h), part(slot, h), sib)

    def z_pass(s):
        low, high = 2 + 2 * s, 3 + 2 * s
        got(f"zp{s}0", part(low, 0))
        move(0, f"zf{s}0", part(low, 0), part(6 + s, 0), zp)
        got(f"zm{s}1", part(high, 1))
        move(0, f"zf{s}1", part(high, 1), part(6 + s, 1), zm)
        share(low, 0)
        share(high, 1)

    def z_near(s):
        low, high = 2 + 2 * s, 3 + 2 * s
        got(f"zp{s}1", part(low, 1))
        share(low, 1)
        got(f"zm{s}0", part(high, 0))
        share(high, 0)

    def z_far(s):
        got(f"zf{s}0", part(6 + s, 0))
        share(6 + s, 0)
        got(f"zf{s}1", part(6 + s, 1))
        share(6 + s, 1)

    def shared(*slots):
        for slot in slots:
            for h in range(2):
                got(f"share{slot}{h}", part(slot, h))

    def block(buf, k, dx=0, h=None):
        at = lax.rem(y + NY - k, NY) * 32
        if h is None:
            rows = pl.ds(pl.multiple_of(at, 32), 32)
        else:
            rows = pl.ds(pl.multiple_of(at + 16 * h, 16), 16)
        return buf.at[lax.rem(x + dx, NX), rows]

    def slab(k):
        whole = wq.at[lax.rem(x + k, NX)]
        move(1, f"slab{k}", whole, whole, sib)

    def over_x(*ks):
        for k in ks:
            for name, device in (("xp", xp), ("xm", xm)):
                move(1, f"{name}{k}", block(wq, k), block(wq, k), device)

    def pass_x(*ks):
        for k in ks:
            got(f"xp{k}", block(wq, k, NX - 1))
            if k < 4:
                move(1, f"xf{k}", block(wq, k, NX - 1), block(wq, k, NX - 1), xp)
            got(f"xm{k}", block(wq, k, 1))
            if k >= 4:
                move(1, f"xf{k}", block(wq, k, 1), block(wq, k, 1), xm)

    def last_x():
        got("xf0", wq.at[lax.rem(x + 2, NX)])
        slab(2)

    def y_first():
        for name, device in (("y1p", y1p), ("y1m", y1m), ("y2p", y2p), ("y2m", y2m)):
            move(1, name, block(wq, 0), block(wq, 0), device)

    def y_pass():
        got("y1p", block(wq, 1))
        move(1, "y3p", block(wq, 1), block(wq, 1), y2p)
        got("y1m", block(wq, 7))
        move(1, "y3m", block(wq, 7), block(wq, 7), y2m)
        got("y2p", block(wq, 2))
        move(1, "y4p", block(wq, 2, 0, 0), block(wq, 2, 0, 0), y2p)
        got("y2m", block(wq, 6))
        move(1, "y4m", block(wq, 6, 0, 1), block(wq, 6, 0, 1), y2m)

    def y_last():
        got("y3p", block(wq, 3))
        got("y3m", block(wq, 5))
        got("y4p", block(wq, 4, 0, 0))
        got("y4m", block(wq, 4, 0, 1))

    def ring(step, dx):
        if step < 4 or dx < 2:
            up = block(wo, step - 1, dx)
            move(1, f"ringp{step}{dx}", up, up, y1p)
        if step < 4 or dx >= 2:
            down = block(wo, (NY + 1 - step) % NY, dx)
            move(1, f"ringm{step}{dx}", down, down, y1m)

    def came(step, dx):
        if step < 4 or dx < 2:
            got(f"ringp{step}{dx}", block(wo, step, dx))
        if step < 4 or dx >= 2:
            got(f"ringm{step}{dx}", block(wo, NY - step, dx))

    def ring_pass(step, *dxs):
        for dx in dxs:
            came(step, dx)
            ring(step + 1, dx)

    def rows_of(k):
        at = pl.multiple_of(lax.rem(y + NY - k, NY) * 32, 32)
        return wo.at[:, pl.ds(at, 32)]

    def rows(*ks):
        for k in ks:
            move(1, f"rows{k}", rows_of(k), rows_of(k), sib)

    def give_own():
        pl.semaphore_wait(hello, 1)
        descriptor("own1", tok_in.at[0, 0], tok.at[1], sib).start()

    @pl.when(core == 0)
    def _():
        arrive(3)
        pl.semaphore_signal(hello, inc=1, device_id=sib, device_id_type=MESH)
        spread(0)
        move(0, "own0", tok_in.at[0, 0], tok.at[0], sib)

    @pl.when(core == 1)
    def _():
        loads = []
        for i, src, buf in ((0, wq_in, wq), (1, wo_in, wo)):
            copy = pltpu.make_async_copy(src, block(buf, 0, 0, zl), near.at[2 + i])
            copy.start()
            loads.append(copy)
        pl.when(zh >= NZ // 2)(give_own)
        arrive(len(across_xy))
        move(1, "pair0", wq_in, block(wq, 0, 0, zl), pair)
        move(1, "pair1", wo_in, block(wo, 0, 0, zl), pair)
        for copy in loads:
            copy.wait()

    for j in range(FRAMES):
        token = lax.broadcasted_iota(jnp.int32, (128, 128), 0) + frames[j] * 128
        hits[:, 128 * j:128 * j + 128] = jnp.where(token == wanted, 1.0, 0.0).T.astype(BF16)
    picked[...] = jnp.zeros_like(picked)

    @pl.when(core == 0)
    def _():
        got("own1", tok.at[1])
        spread(1)

    @pl.when(core == 1)
    def _():
        got("pair0", block(wq, 0, 0, 1 - zl))
        y_first()
        over_x(0)
        got("pair1", block(wo, 0, 0, 1 - zl))
        for dx, device in ((1, xp), (3, xm), (2, x2)):
            move(1, f"ox{dx}", block(wo, 0), block(wo, 0), device)
        ring(1, 0)
        pl.when(zh < NZ // 2)(give_own)
        got("own0", tok.at[0])

    load_tok.wait()
    load_kv.wait()

    def from_x():
        for dx in (1, 3, 2):
            got(f"ox{dx}", block(wo, 0, (NX - dx) % NX))
            ring(1, (NX - dx) % NX)

    def ring_end():
        for dx in range(NX):
            came(4, dx)

    near_order = (0, 3, 1, 2)
    early, late = zh < NZ // 2, zh >= NZ // 2
    first = core == 0
    by_y = [(y_pass,), (over_x, 1, 7, 2, 6), (from_x,), (rows, 0), (pass_x, 0), (ring_pass, 1) + near_order]
    by_y_end = [(y_last,), (over_x, 3, 5, 4), (slab, 0)]
    middle = [(ring_pass, 2) + near_order, (rows, 1, 7), (pass_x, 1, 7, 2, 6), (ring_pass, 3) + near_order, (rows, 2, 6)]
    by_x_end = [(pass_x, 3, 5, 4), (slab, 3), (slab, 1), (rows, 3, 5)]
    finish = [(ring_end,), (rows, 4), (last_x,)]
    events = [
        (first, 2, [(z_pass, 0), (z_near, 0)]),
        (first, 4, [(z_pass, 1), (z_near, 1)]),
        (first, 6, [(z_far, 0)]),
        (first, 7, [(z_far, 1)]),
        (~first, 2, by_y),
        (~first & early, 2, by_y_end + [(ring_pass, 2) + near_order, (rows, 1, 7)]),
        (~first, 2, [(shared, 2)]),
        (~first & late, 3, by_y_end),
        (~first & early, 3, [(pass_x, 1, 7, 2, 6)]),
        (~first, 3, [(shared, 3)]),
        (~first & late, 4, middle),
        (~first & early, 4, [(ring_pass, 3) + near_order, (rows, 2, 6)] + by_x_end),
        (~first, 4, [(shared, 4)]),
        (~first & late, 5, by_x_end),
        (~first, 5, [(shared, 5)]),
        (~first, 6, finish + [(shared, 6)]),
        (~first, 7, [(shared, 7)]),
    ]

    @pl.loop(0, FRAMES)
    def _(t):
        for who, when, calls in events:
            @pl.when(who & (t == when))
            def _(calls=calls):
                for call in calls:
                    call[0](*call[1:])

        at = pl.ds(pl.multiple_of(t * 128, 128), 128)
        kv[at, :] = jnp.dot(tok[t], wkv[...], preferred_element_type=F32).astype(BF16)
        picked[...] += jnp.dot(hits[:, at], tok[t], preferred_element_type=F32)

    @pl.when(core == 0)
    def _():
        got("slab0", wq)

    qs[...] = jnp.dot(picked[...].astype(BF16), wq[...].reshape(1024, 1024), preferred_element_type=F32).astype(BF16)

    scale = 64 ** -0.5 * 1.4426950408889634
    lane = lax.broadcasted_iota(jnp.int32, (128, 256), 1)

    def head(h):
        return (lane >= 64 * h) & (lane < 64 * h + 64)

    def score(n):
        rows = qs[:, 256 * n:256 * n + 256]
        zero = jnp.zeros_like(rows)
        stack = jnp.concatenate([jnp.where(head(h), rows, zero) for h in range(4)], axis=0)
        keys = kv[:, 256 * n:256 * n + 256]
        return lax.dot_general(stack, keys, (((1,), (1,)), ((), ())), preferred_element_type=F32)

    groups = HEADS // 4
    scores[0] = score(0)
    for n in range(groups):
        later = score(n + 1) if n + 1 < groups else None
        now = scores[n % 2]
        peak = jnp.max(now, axis=-1, keepdims=True)
        raw = jnp.exp2((now - peak) * scale)
        total = jnp.sum(raw, axis=-1, keepdims=True)
        values = kv[:, 1024 + 256 * n:1280 + 256 * n]
        mixed = jnp.dot(raw.astype(BF16), values, preferred_element_type=F32) / total
        result = mixed[384:]
        for h in range(3):
            result = jnp.where(head(h), mixed[128 * h:128 * h + 128], result)
        att[:, 256 * n:256 * n + 256] = result.astype(BF16)
        if later is not None:
            scores[(n + 1) % 2] = later

    @pl.when(core == 0)
    def _():
        got("rows0", wo)

    live = lax.broadcasted_iota(jnp.int32, (128, 1024), 0) < counts_ref[0, 0]
    result = jnp.dot(att[...], wo[...].reshape(1024, 1024), preferred_element_type=F32)
    out_ref[0, 0] = (result * jnp.where(live, 1.0, 0.0)).astype(BF16)

    for who in range(2):
        pl.when(core == who)(functools.partial(sent, who))


def local(frame_tokens, w_kv, w_q, w_out, slot_tokens, counts):
    hbm = pl.BlockSpec(memory_space=pl.ANY)
    vmem = pl.BlockSpec(memory_space=pltpu.VMEM)
    return pl.pallas_call(
        kernel,
        out_shape=jax.ShapeDtypeStruct((1, 1, 128, 1024), BF16),
        in_specs=[hbm, hbm, hbm, hbm, vmem, pl.BlockSpec(memory_space=pltpu.SMEM)],
        out_specs=vmem,
        scratch_shapes=[
            pltpu.VMEM((8, 128, 1024), BF16),
            pltpu.VMEM((1024, 2048), BF16),
            pltpu.VMEM((NX, 256, 1024), BF16),
            pltpu.VMEM((NX, 256, 1024), BF16),
            pltpu.VMEM((1024, 2048), BF16),
            pltpu.VMEM((128, 1024), BF16),
            pltpu.VMEM((128, 1024), BF16),
            pltpu.VMEM((128, 1024), F32),
            pltpu.VMEM((128, 1024), BF16),
            pltpu.VMEM((2, 512, 1024), F32),
            pltpu.SemaphoreType.DMA((len(KINDS),)),
            pltpu.SemaphoreType.DMA((SLOTS,)),
            pltpu.SemaphoreType.DMA((4,)),
            pltpu.SemaphoreType.REGULAR,
        ],
        compiler_params=pltpu.CompilerParams(
            collective_id=0, has_side_effects=True, vmem_limit_bytes=56 * 1024 * 1024
        ),
    )(frame_tokens, w_kv, w_q, w_out, slot_tokens, counts)


def solution(mesh):
    placed = (
        P("blk", "win", None, None),
        P(),
        P("win", None),
        P("win", None),
        P(None, "win", None),
        P("blk", "win"),
    )
    return jax.shard_map(
        local, mesh=mesh, in_specs=placed, out_specs=P("blk", "win", None, None), check_vma=False
    )
```

```python
import functools

import jax
import jax.numpy as jnp
from jax import lax
from jax.experimental import pallas as pl
from jax.experimental.pallas import tpu as pltpu
from jax.sharding import PartitionSpec as P

HEADS = 16
FRAMES = 8
NX, NY, NZ = 4, 8, 4
MESH = pl.DeviceIdType.MESH
F32 = jnp.float32
BF16 = jnp.bfloat16

NAMES = ["own0", "own1"]
NAMES += [f"z{_k}{_s}{_h}" for _k in "pmf" for _s in range(2) for _h in range(2)]
NAMES += [f"share{_s}{_h}" for _s in range(2, 8) for _h in range(2)]
NAMES += ["pair0", "pair1", "y1p", "y1m", "y2p", "y2m", "y3p", "y3m", "y4p", "y4m"]
NAMES += [f"x{_k}{_d}" for _k in "pmf" for _d in range(NY)]
NAMES += [f"slab{_k}" for _k in range(NX)]
NAMES += ["ox1", "ox2", "ox3"]
NAMES += [f"ring{_k}{_s}{_d}" for _k in "pm" for _s in range(1, 5) for _d in range(NX)]
NAMES += [f"rows{_k}" for _k in range(NY)]
KINDS = ("own", "z", "share", "pair", "y", "x", "slab", "ox", "ring", "rows")


def kind_of(name):
    for kind in sorted(KINDS, key=len, reverse=True):
        if name.startswith(kind):
            return KINDS.index(kind)


INDEX = {}
for _name in NAMES:
    _key = _name[:2] if _name[:2] == "xf" else _name[:6] if _name[:5] == "share" else _name[:4] if _name[:4] in ("rows", "slab") else _name
    INDEX[_name] = INDEX.setdefault(_key, len(set(INDEX.values())))
SLOTS = max(INDEX.values()) + 1


def kernel(tok_in, wkv_in, wq_in, wo_in, slots_ref, counts_ref, out_ref,
           tok, wkv, wq, wo, kv, qs, att, picked, hits, scores, send, recv, near, hello):
    b = lax.axis_index("blk")
    w = lax.axis_index("win")
    core, zh = lax.rem(b, 2), b // 2
    zl, y, x = lax.rem(w, 2), lax.rem(w // 2, NY), w // (2 * NY)

    def at_z(d):
        return (lax.rem(zh + d, NZ) * 2, w)

    def at_xy(dx, dy, zz):
        return (b, (lax.rem(x + dx, NX) * NY + lax.rem(y + dy, NY)) * 2 + zz)

    sib = (b + 1 - 2 * core, w)
    zp, zm = at_z(1), at_z(NZ - 1)
    pair = at_xy(0, 0, 1 - zl)
    xp, xm, x2 = at_xy(1, 0, zl), at_xy(NX - 1, 0, zl), at_xy(2, 0, zl)
    y1p, y1m = at_xy(0, 1, zl), at_xy(0, NY - 1, zl)
    y2p, y2m = at_xy(0, 2, zl), at_xy(0, NY - 2, zl)

    def descriptor(name, src, dst, device):
        return pltpu.make_async_remote_copy(
            src_ref=src, dst_ref=dst, send_sem=send.at[kind_of(name)], recv_sem=recv.at[INDEX[name]],
            device_id=device, device_id_type=MESH,
        )

    def move(who, name, src, dst, device):
        descriptor(name, src, dst, device).start()

    def got(name, dst):
        descriptor(name, dst, dst, sib).wait_recv()

    def announce(devices):
        barrier = pltpu.get_barrier_semaphore()
        for device in devices:
            pl.semaphore_signal(barrier, inc=1, device_id=device, device_id_type=MESH)

    def arrive(count):
        pl.semaphore_wait(pltpu.get_barrier_semaphore(), count)

    def sent(who):
        kinds = (("own0", tok.at[0]), ("zp00", tok.at[pl.ds(0, 6)]), ("share20", tok.at[pl.ds(0, 6)])) if who == 0 else (
            ("own1", tok.at[0]), ("pair0", wq.at[0, pl.ds(0, 32)]), ("y1p", wq.at[0, pl.ds(0, 224)]),
            ("xp0", wq.at[pl.ds(0, 3)]), ("slab0", wq), ("ox1", wq.at[0, pl.ds(0, 96)]),
            ("ringp10", tok.at[pl.ds(0, 7)]), ("rows0", wo))
        for name, part in kinds:
            descriptor(name, part, part, sib).wait_send()

    across_xy = [pair, xp, xm, x2, y1p, y1m, y2p, y2m]
    pl.when(core == 0)(lambda: announce([zp, zm]))
    pl.when(core == 1)(lambda: announce([sib] + across_xy))

    load_tok = pltpu.make_async_copy(tok_in.at[0, 0], tok.at[core], near.at[0])
    load_tok.start()
    load_kv = pltpu.make_async_copy(wkv_in, wkv, near.at[1])
    load_kv.start()

    before, after, across = lax.rem(zh + NZ - 1, NZ) * 2, lax.rem(zh + 1, NZ) * 2, lax.rem(zh + 2, NZ) * 2
    frames = [2 * zh, 2 * zh + 1, before, after, before + 1, after + 1, across, across + 1]
    wanted = slots_ref[pl.ds(b, 1), 0, :]

    def part(slot, h):
        return tok.at[slot, pl.ds(64 * h, 64)]

    def spread(s):
        for k, h in (("p", 0), ("m", 1), ("p", 1), ("m", 0)):
            src = tok_in.at[0, 0, pl.ds(64 * h, 64)] if s == 0 else part(1, h)
            move(0, f"z{k}{s}{h}", src, part((2 if k == "p" else 3) + 2 * s, h), zp if k == "p" else zm)

    def share(slot, h):
        move(0, f"share{slot}{h}", part(slot, h), part(slot, h), sib)

    def z_pass(s):
        low, high = 2 + 2 * s, 3 + 2 * s
        got(f"zp{s}0", part(low, 0))
        move(0, f"zf{s}0", part(low, 0), part(6 + s, 0), zp)
        got(f"zm{s}1", part(high, 1))
        move(0, f"zf{s}1", part(high, 1), part(6 + s, 1), zm)
        share(low, 0)
        share(high, 1)

    def z_near(s):
        low, high = 2 + 2 * s, 3 + 2 * s
        got(f"zp{s}1", part(low, 1))
        share(low, 1)
        got(f"zm{s}0", part(high, 0))
        share(high, 0)

    def z_far(s):
        got(f"zf{s}0", part(6 + s, 0))
        share(6 + s, 0)
        got(f"zf{s}1", part(6 + s, 1))
        share(6 + s, 1)

    def shared(*slots):
        for slot in slots:
            got(f"share{slot}0", tok.at[slot])

    def block(buf, k, dx=0, h=None):
        at = lax.rem(y + NY - k, NY) * 32
        if h is None:
            rows = pl.ds(pl.multiple_of(at, 32), 32)
        else:
            rows = pl.ds(pl.multiple_of(at + 16 * h, 16), 16)
        return buf.at[lax.rem(x + dx, NX), rows]

    def slab(k):
        whole = wq.at[lax.rem(x + k, NX)]
        move(1, f"slab{k}", whole, whole, sib)

    def over_x(*ks):
        for k in ks:
            for name, device in (("xp", xp), ("xm", xm)):
                move(1, f"{name}{k}", block(wq, k), block(wq, k), device)

    def pass_x(*ks):
        for k in ks:
            got(f"xp{k}", block(wq, k, NX - 1))
            if k < 4:
                move(1, f"xf{k}", block(wq, k, NX - 1), block(wq, k, NX - 1), xp)
            got(f"xm{k}", block(wq, k, 1))
            if k >= 4:
                move(1, f"xf{k}", block(wq, k, 1), block(wq, k, 1), xm)

    def last_x():
        got("xf0", wq.at[lax.rem(x + 2, NX)])
        slab(2)

    def y_first():
        for name, device in (("y1p", y1p), ("y1m", y1m), ("y2p", y2p), ("y2m", y2m)):
            move(1, name, block(wq, 0), block(wq, 0), device)

    def y_pass():
        got("y1p", block(wq, 1))
        move(1, "y3p", block(wq, 1), block(wq, 1), y2p)
        got("y1m", block(wq, 7))
        move(1, "y3m", block(wq, 7), block(wq, 7), y2m)
        got("y2p", block(wq, 2))
        move(1, "y4p", block(wq, 2, 0, 0), block(wq, 2, 0, 0), y2p)
        got("y2m", block(wq, 6))
        move(1, "y4m", block(wq, 6, 0, 1), block(wq, 6, 0, 1), y2m)

    def y_last():
        got("y3p", block(wq, 3))
        got("y3m", block(wq, 5))
        got("y4p", block(wq, 4, 0, 0))
        got("y4m", block(wq, 4, 0, 1))

    def ring(step, dx):
        if step < 4 or dx < 2:
            up = block(wo, step - 1, dx)
            move(1, f"ringp{step}{dx}", up, up, y1p)
        if step < 4 or dx >= 2:
            down = block(wo, (NY + 1 - step) % NY, dx)
            move(1, f"ringm{step}{dx}", down, down, y1m)

    def came(step, dx):
        if step < 4 or dx < 2:
            got(f"ringp{step}{dx}", block(wo, step, dx))
        if step < 4 or dx >= 2:
            got(f"ringm{step}{dx}", block(wo, NY - step, dx))

    def ring_pass(step, *dxs):
        for dx in dxs:
            came(step, dx)
            ring(step + 1, dx)

    def rows_of(k):
        at = pl.multiple_of(lax.rem(y + NY - k, NY) * 32, 32)
        return wo.at[:, pl.ds(at, 32)]

    def rows(*ks):
        for k in ks:
            move(1, f"rows{k}", rows_of(k), rows_of(k), sib)

    def give_own():
        pl.semaphore_wait(hello, 1)
        descriptor("own1", tok_in.at[0, 0], tok.at[1], sib).start()

    @pl.when(core == 0)
    def _():
        arrive(3)
        pl.semaphore_signal(hello, inc=1, device_id=sib, device_id_type=MESH)
        spread(0)
        move(0, "own0", tok_in.at[0, 0], tok.at[0], sib)

    @pl.when(core == 1)
    def _():
        loads = []
        for i, src, buf in ((0, wq_in, wq), (1, wo_in, wo)):
            copy = pltpu.make_async_copy(src, block(buf, 0, 0, zl), near.at[2 + i])
            copy.start()
            loads.append(copy)
        pl.when(zh >= NZ // 2)(give_own)
        arrive(len(across_xy))
        move(1, "pair0", wq_in, block(wq, 0, 0, zl), pair)
        move(1, "pair1", wo_in, block(wo, 0, 0, zl), pair)
        for copy in loads:
            copy.wait()

    for j in range(FRAMES):
        token = lax.broadcasted_iota(jnp.int32, (128, 128), 0) + frames[j] * 128
        hits[:, 128 * j:128 * j + 128] = jnp.where(token == wanted, 1.0, 0.0).T.astype(BF16)
    picked[...] = jnp.zeros_like(picked)

    @pl.when(core == 0)
    def _():
        got("own1", tok.at[1])
        spread(1)

    @pl.when(core == 1)
    def _():
        got("pair0", block(wq, 0, 0, 1 - zl))
        y_first()
        over_x(0)
        got("pair1", block(wo, 0, 0, 1 - zl))
        for dx, device in ((1, xp), (3, xm), (2, x2)):
            move(1, f"ox{dx}", block(wo, 0), block(wo, 0), device)
        ring(1, 0)
        pl.when(zh < NZ // 2)(give_own)

    load_tok.wait()
    load_kv.wait()

    def from_x():
        for dx in (1, 3, 2):
            got(f"ox{dx}", block(wo, 0, (NX - dx) % NX))
            ring(1, (NX - dx) % NX)

    def ring_end():
        for dx in range(NX):
            came(4, dx)

    near_order = (0, 3, 1, 2)
    first = core == 0
    by_y = [(y_pass,), (over_x, 1, 7, 2, 6), (from_x,), (rows, 0)]
    by_y_next = [(pass_x, 0), (ring_pass, 1) + near_order]
    by_y_end = [(y_last,), (over_x, 3, 5, 4), (slab, 0)]
    by_x_end = [(pass_x, 3, 5, 4), (slab, 3), (slab, 1), (rows, 3, 5)]
    finish = [(ring_end,), (rows, 4), (last_x,)]
    events = [
        (first, 2, [(z_pass, 0), (z_near, 0)]),
        (first, 4, [(z_pass, 1), (z_near, 1)]),
        (first, 6, [(z_far, 0)]),
        (first, 7, [(z_far, 1)]),
        (~first, 0, by_y),
        (~first, 0, [(got, "own0", tok.at[0])]),
        (~first, 1, by_y_next),
        (~first, 2, by_y_end + [(ring_pass, 2) + near_order, (rows, 1, 7)]),
        (~first, 2, [(shared, 2)]),
        (~first, 3, [(pass_x, 1, 7, 2, 6)]),
        (~first, 3, [(shared, 3)]),
        (~first, 4, [(ring_pass, 3) + near_order, (rows, 2, 6)] + by_x_end),
        (~first, 4, [(shared, 4)]),
        (~first, 5, [(shared, 5)]),
        (~first, 6, finish + [(shared, 6)]),
        (~first, 7, [(shared, 7)]),
    ]

    @pl.loop(0, FRAMES)
    def _(t):
        for who, when, calls in events:
            @pl.when(who & (t == when))
            def _(calls=calls):
                for call in calls:
                    call[0](*call[1:])

        at = pl.ds(pl.multiple_of(t * 128, 128), 128)
        kv[at, :] = jnp.dot(tok[t], wkv[...], preferred_element_type=F32).astype(BF16)
        picked[...] += jnp.dot(hits[:, at], tok[t], preferred_element_type=F32)

    @pl.when(core == 0)
    def _():
        got("slab0", wq)

    qs[...] = jnp.dot(picked[...].astype(BF16), wq[...].reshape(1024, 1024), preferred_element_type=F32).astype(BF16)

    scale = 64 ** -0.5 * 1.4426950408889634
    lane = lax.broadcasted_iota(jnp.int32, (128, 256), 1)

    def head(h):
        return (lane >= 64 * h) & (lane < 64 * h + 64)

    def score(n):
        rows = qs[:, 256 * n:256 * n + 256]
        zero = jnp.zeros_like(rows)
        stack = jnp.concatenate([jnp.where(head(h), rows, zero) for h in range(4)], axis=0)
        keys = kv[:, 256 * n:256 * n + 256]
        return lax.dot_general(stack, keys, (((1,), (1,)), ((), ())), preferred_element_type=F32)

    groups = HEADS // 4
    scores[0] = score(0)
    for n in range(groups):
        later = score(n + 1) if n + 1 < groups else None
        now = scores[n % 2]
        peak = jnp.max(now, axis=-1, keepdims=True)
        raw = jnp.exp2((now - peak) * scale)
        total = jnp.sum(raw, axis=-1, keepdims=True)
        values = kv[:, 1024 + 256 * n:1280 + 256 * n]
        mixed = jnp.dot(raw.astype(BF16), values, preferred_element_type=F32) / total
        result = mixed[384:]
        for h in range(3):
            result = jnp.where(head(h), mixed[128 * h:128 * h + 128], result)
        att[:, 256 * n:256 * n + 256] = result.astype(BF16)
        if later is not None:
            scores[(n + 1) % 2] = later

    @pl.when(core == 0)
    def _():
        got("rows0", wo)

    live = lax.broadcasted_iota(jnp.int32, (128, 1024), 0) < counts_ref[0, 0]
    result = jnp.dot(att[...], wo[...].reshape(1024, 1024), preferred_element_type=F32)
    out_ref[0, 0] = (result * jnp.where(live, 1.0, 0.0)).astype(BF16)

    for who in range(2):
        pl.when(core == who)(functools.partial(sent, who))


def local(frame_tokens, w_kv, w_q, w_out, slot_tokens, counts):
    hbm = pl.BlockSpec(memory_space=pl.ANY)
    vmem = pl.BlockSpec(memory_space=pltpu.VMEM)
    return pl.pallas_call(
        kernel,
        out_shape=jax.ShapeDtypeStruct((1, 1, 128, 1024), BF16),
        in_specs=[hbm, hbm, hbm, hbm, vmem, pl.BlockSpec(memory_space=pltpu.SMEM)],
        out_specs=vmem,
        scratch_shapes=[
            pltpu.VMEM((8, 128, 1024), BF16),
            pltpu.VMEM((1024, 2048), BF16),
            pltpu.VMEM((NX, 256, 1024), BF16),
            pltpu.VMEM((NX, 256, 1024), BF16),
            pltpu.VMEM((1024, 2048), BF16),
            pltpu.VMEM((128, 1024), BF16),
            pltpu.VMEM((128, 1024), BF16),
            pltpu.VMEM((128, 1024), F32),
            pltpu.VMEM((128, 1024), BF16),
            pltpu.VMEM((2, 512, 1024), F32),
            pltpu.SemaphoreType.DMA((len(KINDS),)),
            pltpu.SemaphoreType.DMA((SLOTS,)),
            pltpu.SemaphoreType.DMA((4,)),
            pltpu.SemaphoreType.REGULAR,
        ],
        compiler_params=pltpu.CompilerParams(
            collective_id=0, has_side_effects=True, vmem_limit_bytes=56 * 1024 * 1024
        ),
    )(frame_tokens, w_kv, w_q, w_out, slot_tokens, counts)


def solution(mesh):
    placed = (
        P("blk", "win", None, None),
        P(),
        P("win", None),
        P("win", None),
        P(None, "win", None),
        P("blk", "win"),
    )
    return jax.shard_map(
        local, mesh=mesh, in_specs=placed, out_specs=P("blk", "win", None, None), check_vma=False
    )
```

```python
import functools

import jax
import jax.numpy as jnp
from jax import lax
from jax.experimental import pallas as pl
from jax.experimental.pallas import tpu as pltpu
from jax.sharding import PartitionSpec as P

HEADS = 16
FRAMES = 8
NX, NY, NZ = 4, 8, 4
MESH = pl.DeviceIdType.MESH
F32 = jnp.float32
BF16 = jnp.bfloat16

NAMES = ["own0", "own1"]
NAMES += [f"z{_k}{_s}{_h}" for _k in "pmf" for _s in range(2) for _h in range(2)]
NAMES += [f"share{_s}{_h}" for _s in range(2, 8) for _h in range(2)]
NAMES += ["pair0", "pair1", "y1p", "y1m", "y2p", "y2m", "y3p", "y3m", "y4p", "y4m"]
NAMES += [f"x{_k}{_d}" for _k in "pmf" for _d in range(NY)]
NAMES += [f"slab{_k}" for _k in range(NX)]
NAMES += ["ox1", "ox2", "ox3"]
NAMES += [f"ring{_k}{_s}{_d}" for _k in "pm" for _s in range(1, 5) for _d in range(NX)]
NAMES += [f"rows{_k}" for _k in range(NY)]
KINDS = ("own", "z", "share", "pair", "y", "x", "slab", "ox", "ring", "rows")


def kind_of(name):
    for kind in sorted(KINDS, key=len, reverse=True):
        if name.startswith(kind):
            return KINDS.index(kind)


INDEX = {}
for _name in NAMES:
    _key = _name[:2] if _name[:2] == "xf" else _name[:6] if _name[:5] == "share" else _name[:4] if _name[:4] in ("rows", "slab") else _name
    INDEX[_name] = INDEX.setdefault(_key, len(set(INDEX.values())))
SLOTS = max(INDEX.values()) + 1


def kernel(tok_in, wkv_in, wq_in, wo_in, slots_ref, counts_ref, out_ref,
           tok, wkv, wq, wo, kv, qs, att, picked, hits, scores, send, recv, near, hello):
    b = lax.axis_index("blk")
    w = lax.axis_index("win")
    core, zh = lax.rem(b, 2), b // 2
    zl, y, x = lax.rem(w, 2), lax.rem(w // 2, NY), w // (2 * NY)

    def at_z(d):
        return (lax.rem(zh + d, NZ) * 2, w)

    def at_xy(dx, dy, zz):
        return (b, (lax.rem(x + dx, NX) * NY + lax.rem(y + dy, NY)) * 2 + zz)

    sib = (b + 1 - 2 * core, w)
    zp, zm = at_z(1), at_z(NZ - 1)
    pair = at_xy(0, 0, 1 - zl)
    xp, xm, x2 = at_xy(1, 0, zl), at_xy(NX - 1, 0, zl), at_xy(2, 0, zl)
    y1p, y1m = at_xy(0, 1, zl), at_xy(0, NY - 1, zl)
    y2p, y2m = at_xy(0, 2, zl), at_xy(0, NY - 2, zl)

    def descriptor(name, src, dst, device):
        return pltpu.make_async_remote_copy(
            src_ref=src, dst_ref=dst, send_sem=send.at[kind_of(name)], recv_sem=recv.at[INDEX[name]],
            device_id=device, device_id_type=MESH,
        )

    def move(who, name, src, dst, device):
        descriptor(name, src, dst, device).start()

    def got(name, dst):
        descriptor(name, dst, dst, sib).wait_recv()

    def announce(devices):
        barrier = pltpu.get_barrier_semaphore()
        for device in devices:
            pl.semaphore_signal(barrier, inc=1, device_id=device, device_id_type=MESH)

    def arrive(count):
        pl.semaphore_wait(pltpu.get_barrier_semaphore(), count)

    def sent(who):
        kinds = (("own0", tok.at[0]), ("zp00", tok.at[pl.ds(0, 6)]), ("share20", tok.at[pl.ds(0, 6)])) if who == 0 else (
            ("own1", tok.at[0]), ("pair0", wq.at[0, pl.ds(0, 32)]), ("y1p", wq.at[0, pl.ds(0, 224)]),
            ("xp0", wq.at[pl.ds(0, 3)]), ("slab0", wq), ("ox1", wq.at[0, pl.ds(0, 96)]),
            ("ringp10", tok.at[pl.ds(0, 7)]), ("rows0", wo))
        for name, part in kinds:
            descriptor(name, part, part, sib).wait_send()

    across_xy = [pair, xp, xm, x2, y1p, y1m, y2p, y2m]
    pl.when(core == 0)(lambda: announce([zp, zm]))
    pl.when(core == 1)(lambda: announce([sib] + across_xy))

    load_tok = pltpu.make_async_copy(tok_in.at[0, 0], tok.at[core], near.at[0])
    load_tok.start()
    load_kv = pltpu.make_async_copy(wkv_in, wkv, near.at[1])
    load_kv.start()

    before, after, across = lax.rem(zh + NZ - 1, NZ) * 2, lax.rem(zh + 1, NZ) * 2, lax.rem(zh + 2, NZ) * 2
    frames = [2 * zh, 2 * zh + 1, before, after, before + 1, after + 1, across, across + 1]
    wanted = slots_ref[pl.ds(b, 1), 0, :]

    def part(slot, h):
        return tok.at[slot, pl.ds(64 * h, 64)]

    def spread(s):
        for k, h in (("p", 0), ("m", 1), ("p", 1), ("m", 0)):
            src = tok_in.at[0, 0, pl.ds(64 * h, 64)] if s == 0 else part(1, h)
            move(0, f"z{k}{s}{h}", src, part((2 if k == "p" else 3) + 2 * s, h), zp if k == "p" else zm)

    def share(slot, h):
        move(0, f"share{slot}{h}", part(slot, h), part(slot, h), sib)

    def z_pass(s):
        low, high = 2 + 2 * s, 3 + 2 * s
        got(f"zp{s}0", part(low, 0))
        move(0, f"zf{s}0", part(low, 0), part(6 + s, 0), zp)
        got(f"zm{s}1", part(high, 1))
        move(0, f"zf{s}1", part(high, 1), part(6 + s, 1), zm)
        share(low, 0)
        share(high, 1)

    def z_near(s):
        low, high = 2 + 2 * s, 3 + 2 * s
        got(f"zp{s}1", part(low, 1))
        share(low, 1)
        got(f"zm{s}0", part(high, 0))
        share(high, 0)

    def z_far(s):
        got(f"zf{s}0", part(6 + s, 0))
        share(6 + s, 0)
        got(f"zf{s}1", part(6 + s, 1))
        share(6 + s, 1)

    def shared(*slots):
        for slot in slots:
            got(f"share{slot}0", tok.at[slot])

    def block(buf, k, dx=0, h=None):
        at = lax.rem(y + NY - k, NY) * 32
        if h is None:
            rows = pl.ds(pl.multiple_of(at, 32), 32)
        else:
            rows = pl.ds(pl.multiple_of(at + 16 * h, 16), 16)
        return buf.at[lax.rem(x + dx, NX), rows]

    def slab(k):
        whole = wq.at[lax.rem(x + k, NX)]
        move(1, f"slab{k}", whole, whole, sib)

    def over_x(*ks):
        for k in ks:
            for name, device in (("xp", xp), ("xm", xm)):
                move(1, f"{name}{k}", block(wq, k), block(wq, k), device)

    def pass_x(*ks):
        for k in ks:
            got(f"xp{k}", block(wq, k, NX - 1))
            if k < 4:
                move(1, f"xf{k}", block(wq, k, NX - 1), block(wq, k, NX - 1), xp)
            got(f"xm{k}", block(wq, k, 1))
            if k >= 4:
                move(1, f"xf{k}", block(wq, k, 1), block(wq, k, 1), xm)

    def last_x():
        got("xf0", wq.at[lax.rem(x + 2, NX)])
        slab(2)

    def y_first():
        for name, device in (("y1p", y1p), ("y1m", y1m), ("y2p", y2p), ("y2m", y2m)):
            move(1, name, block(wq, 0), block(wq, 0), device)

    def y_pass():
        got("y1p", block(wq, 1))
        move(1, "y3p", block(wq, 1), block(wq, 1), y2p)
        got("y1m", block(wq, 7))
        move(1, "y3m", block(wq, 7), block(wq, 7), y2m)
        got("y2p", block(wq, 2))
        move(1, "y4p", block(wq, 2, 0, 0), block(wq, 2, 0, 0), y2p)
        got("y2m", block(wq, 6))
        move(1, "y4m", block(wq, 6, 0, 1), block(wq, 6, 0, 1), y2m)

    def y_last():
        got("y3p", block(wq, 3))
        got("y3m", block(wq, 5))
        got("y4p", block(wq, 4, 0, 0))
        got("y4m", block(wq, 4, 0, 1))

    def ring(step, dx):
        if step < 4 or dx < 2:
            up = block(wo, step - 1, dx)
            move(1, f"ringp{step}{dx}", up, up, y1p)
        if step < 4 or dx >= 2:
            down = block(wo, (NY + 1 - step) % NY, dx)
            move(1, f"ringm{step}{dx}", down, down, y1m)

    def came(step, dx):
        if step < 4 or dx < 2:
            got(f"ringp{step}{dx}", block(wo, step, dx))
        if step < 4 or dx >= 2:
            got(f"ringm{step}{dx}", block(wo, NY - step, dx))

    def ring_pass(step, *dxs):
        for dx in dxs:
            came(step, dx)
            ring(step + 1, dx)

    def rows_of(k):
        at = pl.multiple_of(lax.rem(y + NY - k, NY) * 32, 32)
        return wo.at[:, pl.ds(at, 32)]

    def rows(*ks):
        for k in ks:
            move(1, f"rows{k}", rows_of(k), rows_of(k), sib)

    def give_own():
        pl.semaphore_wait(hello, 1)
        descriptor("own1", tok_in.at[0, 0], tok.at[1], sib).start()

    @pl.when(core == 0)
    def _():
        arrive(3)
        pl.semaphore_signal(hello, inc=1, device_id=sib, device_id_type=MESH)
        spread(0)
        move(0, "own0", tok_in.at[0, 0], tok.at[0], sib)

    @pl.when(core == 1)
    def _():
        loads = []
        for i, src, buf in ((0, wq_in, wq), (1, wo_in, wo)):
            copy = pltpu.make_async_copy(src, block(buf, 0, 0, zl), near.at[2 + i])
            copy.start()
            loads.append(copy)
        pl.when(zh >= NZ // 2)(give_own)
        arrive(len(across_xy))
        move(1, "pair0", wq_in, block(wq, 0, 0, zl), pair)
        move(1, "pair1", wo_in, block(wo, 0, 0, zl), pair)
        for copy in loads:
            copy.wait()

    for j in range(FRAMES):
        token = lax.broadcasted_iota(jnp.int32, (128, 128), 0) + frames[j] * 128
        hits[:, 128 * j:128 * j + 128] = jnp.where(token == wanted, 1.0, 0.0).T.astype(BF16)
    picked[...] = jnp.zeros_like(picked)

    @pl.when(core == 0)
    def _():
        got("own1", tok.at[1])
        spread(1)

    @pl.when(core == 1)
    def _():
        got("pair0", block(wq, 0, 0, 1 - zl))
        y_first()
        over_x(0)
        got("pair1", block(wo, 0, 0, 1 - zl))
        for dx, device in ((1, xp), (3, xm), (2, x2)):
            move(1, f"ox{dx}", block(wo, 0), block(wo, 0), device)
        ring(1, 0)
        pl.when(zh < NZ // 2)(give_own)

    load_tok.wait()
    load_kv.wait()

    def from_x():
        for dx in (1, 3, 2):
            got(f"ox{dx}", block(wo, 0, (NX - dx) % NX))
            ring(1, (NX - dx) % NX)

    def ring_end():
        for dx in range(NX):
            came(4, dx)

    near_order = (0, 3, 1, 2)
    first = core == 0
    by_y = [(y_pass,), (over_x, 1, 7, 2, 6), (from_x,), (rows, 0)]
    by_y_next = [(pass_x, 0), (ring_pass, 1) + near_order]
    by_y_end = [(y_last,), (over_x, 3, 5, 4), (slab, 0)]
    by_x_end = [(pass_x, 3, 5, 4), (slab, 3), (slab, 1), (rows, 3, 5)]
    finish = [(ring_end,), (rows, 4), (last_x,)]
    events = [
        (first, 2, [(z_pass, 0), (z_near, 0)]),
        (first, 4, [(z_pass, 1), (z_near, 1)]),
        (first, 6, [(z_far, 0)]),
        (first, 7, [(z_far, 1)]),
        (~first, 2, by_y_next),
        (~first, 2, by_y_end + [(ring_pass, 2) + near_order, (rows, 1, 7)]),
        (~first, 2, [(shared, 2)]),
        (~first, 3, [(pass_x, 1, 7, 2, 6)]),
        (~first, 3, [(shared, 3)]),
        (~first, 4, [(ring_pass, 3) + near_order, (rows, 2, 6)] + by_x_end),
        (~first, 4, [(shared, 4)]),
        (~first, 5, [(shared, 5)]),
        (~first, 6, finish + [(shared, 6)]),
        (~first, 7, [(shared, 7)]),
    ]

    @pl.when(~first)
    def _():
        for call in by_y:
            call[0](*call[1:])
        got("own0", tok.at[0])

    pair_rows = tok[0:2].reshape(256, 1024)
    kv[0:256, :] = jnp.dot(pair_rows, wkv[...], preferred_element_type=F32).astype(BF16)
    picked[...] += jnp.dot(hits[:, 0:256], pair_rows, preferred_element_type=F32)

    @pl.loop(2, FRAMES)
    def _(t):
        for who, when, calls in events:
            @pl.when(who & (t == when))
            def _(calls=calls):
                for call in calls:
                    call[0](*call[1:])

        at = pl.ds(pl.multiple_of(t * 128, 128), 128)
        kv[at, :] = jnp.dot(tok[t], wkv[...], preferred_element_type=F32).astype(BF16)
        picked[...] += jnp.dot(hits[:, at], tok[t], preferred_element_type=F32)

    @pl.when(core == 0)
    def _():
        got("slab0", wq)

    qs[...] = jnp.dot(picked[...].astype(BF16), wq[...].reshape(1024, 1024), preferred_element_type=F32).astype(BF16)

    scale = 64 ** -0.5 * 1.4426950408889634
    lane = lax.broadcasted_iota(jnp.int32, (128, 256), 1)

    def head(h):
        return (lane >= 64 * h) & (lane < 64 * h + 64)

    def score(n):
        rows = qs[:, 256 * n:256 * n + 256]
        zero = jnp.zeros_like(rows)
        stack = jnp.concatenate([jnp.where(head(h), rows, zero) for h in range(4)], axis=0)
        keys = kv[:, 256 * n:256 * n + 256]
        return lax.dot_general(stack, keys, (((1,), (1,)), ((), ())), preferred_element_type=F32)

    groups = HEADS // 4
    scores[0] = score(0)
    for n in range(groups):
        later = score(n + 1) if n + 1 < groups else None
        now = scores[n % 2]
        peak = jnp.max(now, axis=-1, keepdims=True)
        raw = jnp.exp2((now - peak) * scale)
        total = jnp.sum(raw, axis=-1, keepdims=True)
        values = kv[:, 1024 + 256 * n:1280 + 256 * n]
        mixed = jnp.dot(raw.astype(BF16), values, preferred_element_type=F32) / total
        result = mixed[384:]
        for h in range(3):
            result = jnp.where(head(h), mixed[128 * h:128 * h + 128], result)
        att[:, 256 * n:256 * n + 256] = result.astype(BF16)
        if later is not None:
            scores[(n + 1) % 2] = later

    @pl.when(core == 0)
    def _():
        got("rows0", wo)

    live = lax.broadcasted_iota(jnp.int32, (128, 1024), 0) < counts_ref[0, 0]
    result = jnp.dot(att[...], wo[...].reshape(1024, 1024), preferred_element_type=F32)
    out_ref[0, 0] = (result * jnp.where(live, 1.0, 0.0)).astype(BF16)

    for who in range(2):
        pl.when(core == who)(functools.partial(sent, who))


def local(frame_tokens, w_kv, w_q, w_out, slot_tokens, counts):
    hbm = pl.BlockSpec(memory_space=pl.ANY)
    vmem = pl.BlockSpec(memory_space=pltpu.VMEM)
    return pl.pallas_call(
        kernel,
        out_shape=jax.ShapeDtypeStruct((1, 1, 128, 1024), BF16),
        in_specs=[hbm, hbm, hbm, hbm, vmem, pl.BlockSpec(memory_space=pltpu.SMEM)],
        out_specs=vmem,
        scratch_shapes=[
            pltpu.VMEM((8, 128, 1024), BF16),
            pltpu.VMEM((1024, 2048), BF16),
            pltpu.VMEM((NX, 256, 1024), BF16),
            pltpu.VMEM((NX, 256, 1024), BF16),
            pltpu.VMEM((1024, 2048), BF16),
            pltpu.VMEM((128, 1024), BF16),
            pltpu.VMEM((128, 1024), BF16),
            pltpu.VMEM((128, 1024), F32),
            pltpu.VMEM((128, 1024), BF16),
            pltpu.VMEM((2, 512, 1024), F32),
            pltpu.SemaphoreType.DMA((len(KINDS),)),
            pltpu.SemaphoreType.DMA((SLOTS,)),
            pltpu.SemaphoreType.DMA((4,)),
            pltpu.SemaphoreType.REGULAR,
        ],
        compiler_params=pltpu.CompilerParams(
            collective_id=0, has_side_effects=True, vmem_limit_bytes=56 * 1024 * 1024
        ),
    )(frame_tokens, w_kv, w_q, w_out, slot_tokens, counts)


def solution(mesh):
    placed = (
        P("blk", "win", None, None),
        P(),
        P("win", None),
        P("win", None),
        P(None, "win", None),
        P("blk", "win"),
    )
    return jax.shard_map(
        local, mesh=mesh, in_specs=placed, out_specs=P("blk", "win", None, None), check_vma=False
    )
```
